128 devices in a mesh: wide: 16 (over x, y), narrow: 8 (over z, core).
Axes of the slice: x: 4, y: 4, z: 4, core: 2. Of those that a mesh axis runs over, the one named last changes fastest.
Arguments:
- old_field: float32 [4096, 128, 128], P(('wide', 'narrow')), may hold values from -6 to 6
- old_level: int32 [4096], P(('wide', 'narrow')), may hold values from 0 to 1
- new_source: int32 [32, 32], P('wide', 'narrow'), may hold values from 0 to 4095, as said below
- stretch_coef: float32 [8192, 8192], P('wide', 'narrow'), may hold values from 0.2 to 2
- bend_coef: float32 [8192, 8192], P('wide', 'narrow'), may hold values from 0.05 to 0.5
- load_field: float32 [8192, 8192], P('wide', 'narrow'), may hold values from -6 to 6
Outputs:
- relaxed: float32 [8192, 8192], P('wide', 'narrow')
The draws below stay inside these ranges and needn't reach their ends.
Inputs may be any that keep to these rules, and one draw needn't show every extreme that they name: new_source names an old block held by a device with the same narrow index; one old device gives at most 2 sibling groups to one new device, and exactly 2 wherever it gives any.
All inputs are finite; a program needn't handle non-finite values.
Results may differ from the reference program's by a relative error of at most 0.0001.
Values sent between devices are 32-bit elements; how exact they have to be, the bound alone decides.
No kernel may reach another device: no remote copies, remote signals or barrier semaphores. Data moves between devices by JAX's collectives and lax.ppermute only.
A program may use at most 128 MiB of HBM per device.

```python
import math
import jax
import jax.numpy as jnp
from jax import lax

BS = 128
BX_DEV = 4
BY_DEV = 8
SWEEPS = 2
BLK_DEV = 32
RANKS = 16
SEGS = 8
CAP = 2
NOLD = 4096
NGX = 32
NGY = 32
NX = 8192
NY = 8192


def draw_new_source(key, part):
    group_rows = BX_DEV // 2
    group_cols = BY_DEV // 2
    group_x = jnp.arange(NGX, dtype=jnp.int32)[:, None]
    group_y = jnp.arange(NGY, dtype=jnp.int32)[None, :]
    rank_w = group_x // group_rows
    seg_n = group_y // group_cols
    local_k = group_x % group_rows * group_cols + group_y % group_cols
    group_id = local_k // CAP
    scores = jax.random.randint(jax.random.fold_in(key, 12), (RANKS, SEGS, RANKS), 0, 1 << 20, dtype=jnp.int32)
    scores = scores * RANKS + jnp.arange(RANKS, dtype=jnp.int32)[None, None, :]
    shuffle = jnp.argsort(scores, axis=-1, stable=True).astype(jnp.int32)
    offset = shuffle[rank_w, seg_n, group_id]
    from_rank = (rank_w + offset) % RANKS
    from_local = jax.random.randint(jax.random.fold_in(key, 13), (NGX, NGY), 0, BLK_DEV, dtype=jnp.int32)
    return ((from_rank * SEGS + seg_n) * BLK_DEV + from_local).astype(jnp.int32)


def touch_ends(array, own_key, least, high):
    index_at = [jax.random.randint(jax.random.fold_in(own_key, axis), (), 0, length) for axis, length in enumerate(array.shape)]
    widest = array.shape.index(max(array.shape))
    beside = index_at[:widest] + [(index_at[widest] + 1) % array.shape[widest]] + index_at[widest + 1:]
    return array.at[tuple(index_at)].set(least).at[tuple(beside)].set(high)


def shard_levels(stream_key, extent, pieces, smallest, top_value):
    level = 1.0
    for dim, parts in pieces:
        draws = jax.random.uniform(jax.random.fold_in(jax.random.fold_in(stream_key, 6), dim), (parts,), jnp.float32, smallest / len(pieces), top_value / len(pieces))
        level = level * jnp.repeat(jnp.exp(draws), extent[dim] // parts).reshape((-1,) + (1,) * (len(extent) - 1 - dim))
    return level


def gaussian(stream_key, shape, scale, reach, shards=(), kind=jnp.bfloat16):
    result = scale * jax.random.normal(stream_key, shape, jnp.float32)
    if shards:
        result = result * shard_levels(stream_key, shape, shards, -0.22, 0.18)
    return jnp.clip(result, -reach, reach).astype(kind)


def setup_inputs(seed: int = 0) -> dict:
    seeds = jax.random.split(jax.random.key(seed), 7)
    return {
        "old_field": gaussian(seeds[0], (NOLD, BS, BS), 1.0, 6.0, ((0, 128),), jnp.float32),
        "old_level": touch_ends(jax.random.randint(seeds[1], (NOLD,), 0, 2), jax.random.fold_in(seeds[1], 1), 0, 1).astype(jnp.int32),
        "new_source": draw_new_source(jax.random.fold_in(seeds[6], 71), 0),
        "stretch_coef": jnp.clip(jnp.exp(math.log(2.0) - 2.3025851 * jax.random.uniform(seeds[3], (NX, NY), jnp.float32) ** shard_levels(seeds[3], (NX, NY), ((0, 16), (1, 8)), -0.2, 0.2)), 0.2, 2.0),
        "bend_coef": jnp.clip(jnp.exp(math.log(0.5) - 2.3025851 * jax.random.uniform(seeds[4], (NX, NY), jnp.float32) ** shard_levels(seeds[4], (NX, NY), ((0, 16), (1, 8)), -0.2, 0.2)), 0.05, 0.5),
        "load_field": gaussian(seeds[5], (NX, NY), 1.0, 6.0, ((0, 16), (1, 8)), jnp.float32),
    }


OMEGA = 0.5


def quadrant_table(side_cells, half_index):
    half_size = side_cells // 2
    row_ids = jnp.arange(side_cells, dtype=jnp.int32)[:, None]
    col_ids = jnp.arange(side_cells, dtype=jnp.int32)[None, :]
    base_cell = half_index * half_size
    near_cell = base_cell + row_ids // 2
    other_cell = near_cell + jnp.where(row_ids % 2 == 1, 1, -1)
    other_cell = jnp.clip(other_cell, base_cell, base_cell + half_size - 1)
    return 0.75 * (col_ids == near_cell).astype(jnp.float32) + 0.25 * (col_ids == other_cell).astype(jnp.float32)


def refine_group(parents):
    side_cells = parents.shape[-1]
    tables = [quadrant_table(side_cells, 0), quadrant_table(side_cells, 1)]
    upper = [jnp.einsum("ij,njk->nik", table, parents, precision=lax.Precision.HIGHEST) for table in tables]
    rows_out = []
    for half_x in range(2):
        pair = [jnp.einsum("nik,lk->nil", upper[half_x], tables[half_y], precision=lax.Precision.HIGHEST) for half_y in range(2)]
        rows_out.append(jnp.stack(pair, axis=1))
    return jnp.stack(rows_out, axis=1)


def spacing_factor(levels):
    return 1.0 + 3.0 * (levels >= 1).astype(jnp.float32)


def relax(field_pad, stretch_pad, bend_pad, load_core, inside):
    center = field_pad[2:-2, 2:-2]
    laplace = field_pad[:-2, 1:-1] + field_pad[2:, 1:-1] + field_pad[1:-1, :-2] + field_pad[1:-1, 2:] - 4.0 * field_pad[1:-1, 1:-1]
    moment = bend_pad * laplace
    bending = moment[:-2, 1:-1] + moment[2:, 1:-1] + moment[1:-1, :-2] + moment[1:-1, 2:] - 4.0 * moment[1:-1, 1:-1]
    stretch_mid = stretch_pad[1:-1, 1:-1]
    diagonal = 16.0 * bend_pad[1:-1, 1:-1]
    stretching = jnp.zeros_like(center)
    neighbours = (
        (stretch_pad[:-2, 1:-1], bend_pad[:-2, 1:-1], field_pad[1:-3, 2:-2]),
        (stretch_pad[2:, 1:-1], bend_pad[2:, 1:-1], field_pad[3:-1, 2:-2]),
        (stretch_pad[1:-1, :-2], bend_pad[1:-1, :-2], field_pad[2:-2, 1:-3]),
        (stretch_pad[1:-1, 2:], bend_pad[1:-1, 2:], field_pad[2:-2, 3:-1]),
    )
    for near_stretch, near_bend, near_field in neighbours:
        face_coef = 0.5 * (stretch_mid + near_stretch)
        stretching = stretching + face_coef * (center - near_field)
        diagonal = diagonal + face_coef + near_bend
    remainder = load_core - (stretching + bending)
    if inside is None:
        return center + OMEGA * remainder / diagonal
    safe_diag = jnp.where(inside, diagonal, 1.0)
    return jnp.where(inside, center + OMEGA * remainder / safe_diag, 0.0)


def reference(old_field, old_level, new_source, stretch_coef, bend_coef, load_field):
    flat_source = new_source.reshape(-1)
    children = refine_group(old_field[flat_source])
    spacing = spacing_factor(old_level[flat_source])
    grid_field = children.reshape(NGX, NGY, 2, 2, BS, BS).transpose(0, 2, 4, 1, 3, 5).reshape(NX, NY)
    scale_grid = jnp.repeat(jnp.repeat(spacing.reshape(NGX, NGY), 2 * BS, axis=0), 2 * BS, axis=1)
    stretch_eff = stretch_coef * scale_grid
    bend_eff = bend_coef * scale_grid * scale_grid
    stretch_pad = jnp.pad(stretch_eff, 1)
    bend_pad = jnp.pad(bend_eff, 1)
    for sweep_index in range(SWEEPS):
        grid_field = relax(jnp.pad(grid_field, 2), stretch_pad, bend_pad, load_field, None)
    return grid_field
```

```python
import functools

import jax
import jax.numpy as jnp
from jax import lax
from jax.experimental import pallas as pl
from jax.experimental.pallas import tpu as pltpu
from jax.sharding import PartitionSpec as P

SWEEPS = 2
OMEGA = 0.5
BS = 128
TOP = 16
F32 = jnp.float32
VMEM = pl.BlockSpec(memory_space=pltpu.VMEM)
SMEM = pl.BlockSpec(memory_space=pltpu.SMEM)
ANY = pl.BlockSpec(memory_space=pl.ANY)
HBM = pl.BlockSpec(memory_space=pltpu.HBM)


def lanes():
    return lax.broadcasted_iota(jnp.int32, (8, BS), 1)


def subs():
    return lax.broadcasted_iota(jnp.int32, (8, BS), 0)


def slot_of(owners, position):
    hit = jnp.int32(0)
    for earlier in range(position):
        hit = hit | (owners[earlier] == owners[position]).astype(jnp.int32)
    return hit


def send_kernel(dims, table, field, out, strip, sems, strip_sem):
    ranks, groups, per_device, segments = dims
    me = lax.axis_index("wide")
    first, last, wanted = [], [], []
    for w in range(ranks):
        low, high, any_hit = jnp.int32(0), jnp.int32(0), jnp.int32(0)
        for g in range(groups):
            source = table[w, g]
            local = lax.rem(source, per_device)
            hit = lax.div(source, per_device * segments) == me
            high = jnp.where(hit, local, high)
            any_hit = jnp.where(hit, 1, any_hit)
        for g in reversed(range(groups)):
            source = table[w, g]
            local = lax.rem(source, per_device)
            hit = lax.div(source, per_device * segments) == me
            low = jnp.where(hit, local, low)
        first.append(low)
        last.append(high)
        wanted.append(any_hit)

        @pl.when(any_hit == 1)
        def _():
            for slot, local in ((0, low), (1, high)):
                pltpu.make_async_copy(
                    field.at[local], out.at[w, pl.ds(slot * BS, BS), :], sems.at[w, slot]
                ).start()

    sub = subs()
    for w in range(ranks):
        up, down = max(w - 1, 0), min(w + 1, ranks - 1)
        strip[w, 0:8, :] = jnp.where(
            sub < 4,
            pltpu.roll(field[first[up], BS - 8 : BS, :], 4, 0),
            field[last[up], BS - 8 : BS, :],
        )
        strip[w, 8:16, :] = jnp.where(
            sub < 4,
            field[first[down], 0:8, :],
            pltpu.roll(field[last[down], 0:8, :], 4, 0),
        )
    copy = pltpu.make_async_copy(strip, out.at[:, 2 * BS : 2 * BS + 16, :], strip_sem)
    copy.start()
    for w in range(ranks):

        @pl.when(wanted[w] == 1)
        def _():
            for slot in range(2):
                pltpu.make_async_copy(
                    field.at[0], out.at[w, pl.ds(slot * BS, BS), :], sems.at[w, slot]
                ).wait()

    copy.wait()


def take_kernel(dims, table, recv, left, middle, right, tiles, sems, tile_sems):
    ranks, groups, per_device, segments = dims
    gy_count = groups // 2
    me = lax.axis_index("wide")
    up, down = jnp.maximum(me - 1, 0), jnp.minimum(me + 1, ranks - 1)

    def owners_of(row):
        return [lax.div(table[row, g], per_device * segments) for g in range(groups)]

    mine, above, below = owners_of(me), owners_of(up), owners_of(down)

    def column(gy):
        if gy == 0:
            return left
        if gy == gy_count - 1:
            return right
        return middle.at[gy - 1]

    copies = []
    for gx in range(2):
        for gy in range(gy_count):
            g = gx * gy_count + gy
            start = pl.multiple_of(slot_of(mine, g) * BS, BS)
            copies.append(
                pltpu.make_async_copy(
                    recv.at[mine[g], pl.ds(start, BS), :],
                    column(gy).at[8 + gx * BS : 8 + (gx + 1) * BS, :],
                    sems.at[g],
                )
            )
    for gy in range(gy_count):
        copies.append(
            pltpu.make_async_copy(
                recv.at[above[gy_count + gy], 2 * BS : 2 * BS + 8, :],
                tiles.at[gy],
                tile_sems.at[gy],
            )
        )
        copies.append(
            pltpu.make_async_copy(
                recv.at[below[gy], 2 * BS + 8 : 2 * BS + 16, :],
                tiles.at[gy_count + gy],
                tile_sems.at[gy_count + gy],
            )
        )
    for copy in copies:
        copy.start()
    for copy in copies:
        copy.wait()
    for gy in range(gy_count):
        tile = tiles[gy]
        tile = jnp.where(slot_of(above, gy_count + gy) == 0, pltpu.roll(tile, 4, 0), tile)
        column(gy)[0:8, :] = jnp.where(me > 0, tile, 0.0)
        tile = tiles[gy_count + gy]
        tile = jnp.where(slot_of(below, gy) == 1, pltpu.roll(tile, 4, 0), tile)
        column(gy)[8 + 2 * BS : 16 + 2 * BS, :] = jnp.where(me < ranks - 1, tile, 0.0)


def scale_kernel(dims, table, a_in, b_in, l_in, above, below, a_out, b_out, l_out, to_left, to_right):
    ranks, groups, per_device, segments = dims
    gy_count = groups // 2
    planes = 2 * gy_count
    me = lax.axis_index("wide")
    rows = a_in.shape[0]

    def spacing(row, g):
        source = table[row, g]
        level = table[lax.div(source, per_device * segments), groups + lax.rem(source, per_device)]
        return jnp.where(level >= 1, F32(4.0), F32(1.0))

    lane = lanes()

    def put(row, c, a, b, l):
        a_out[c, pl.ds(row, 8), :] = a
        b_out[c, pl.ds(row, 8), :] = b
        l_out[c, pl.ds(row, 8), :] = l
        if c == 0:
            to_left[pl.ds(row, 8), :] = jnp.where(
                lane < 3,
                a,
                jnp.where(lane < 6, pltpu.roll(b, 3, 1), pltpu.roll(l, 6, 1)),
            )
        if c == planes - 1:
            to_right[pl.ds(row, 8), :] = jnp.where(
                lane >= BS - 3,
                a,
                jnp.where(lane >= BS - 6, pltpu.roll(b, BS - 3, 1), pltpu.roll(l, BS - 6, 1)),
            )

    up, down = jnp.maximum(me - 1, 0), jnp.minimum(me + 1, ranks - 1)
    half = rows // 2
    for gx in range(2):
        factors = [spacing(me, gx * gy_count + gy) for gy in range(gy_count)]

        def step(k, carry):
            row = pl.multiple_of(gx * half + k * 8, 8)
            for c in range(planes):
                s = factors[c // 2]
                cols = slice(c * BS, (c + 1) * BS)
                put(
                    pl.multiple_of(row + TOP, 8),
                    c,
                    a_in[pl.ds(row, 8), cols] * s,
                    b_in[pl.ds(row, 8), cols] * (s * s),
                    l_in[pl.ds(row, 8), cols],
                )
            return carry

        lax.fori_loop(0, half // 8, step, 0)
    for c in range(planes):
        cols = slice(c * BS, (c + 1) * BS)
        s = spacing(up, gy_count + c // 2)
        tile = above[:, cols]
        put(TOP - 8, c, pltpu.roll(tile, 5, 0) * s, pltpu.roll(tile, 2, 0) * (s * s), tile)
        s = spacing(down, c // 2)
        tile = below[:, cols]
        put(TOP + rows, c, tile * s, pltpu.roll(tile, 5, 0) * (s * s), pltpu.roll(tile, 2, 0))


def coef_kernel(dims, a, b, l, from_right, from_left, b8, l8, fx, fy, wt, a8):
    ranks, groups, per_device, segments = dims
    planes = groups
    me, seg = lax.axis_index("wide"), lax.axis_index("narrow")
    rows = a.shape[1] - 2 * TOP
    lane, sub = lanes(), subs()
    strips = rows // 8 + 2

    def side(k, carry):
        row = pl.multiple_of(TOP - 8 + 8 * k, 8)
        z = jnp.where(lane < BS // 2, from_right[pl.ds(row, 8), :], from_left[pl.ds(row, 8), :])
        near = lane < BS // 2
        a8[pl.ds(row, 8), :] = z
        b8[pl.ds(row, 8), :] = jnp.where(near, pltpu.roll(z, BS - 3, 1), pltpu.roll(z, 3, 1))
        l8[pl.ds(row, 8), :] = jnp.where(near, pltpu.roll(z, BS - 6, 1), pltpu.roll(z, 6, 1))
        return carry

    lax.fori_loop(0, strips, side, 0, unroll=2)
    side_ok = ((lane < 2) & (seg < segments - 1)) | ((lane >= BS - 2) & (seg > 0))

    def plane(ref, ref8, c, start):
        return ref8[pl.ds(start, 8), :] if c == planes else ref[c, pl.ds(start, 8), :]

    def step(k, carry):
        row = pl.multiple_of(TOP - 8 + 8 * k, 8)
        at = [plane(a, a8, c, row) for c in range(planes + 1)]
        bt = [plane(b, b8, c, row) for c in range(planes + 1)]
        at_r = [pltpu.roll(t, BS - 1, 1) for t in at]
        bt_r = [pltpu.roll(t, BS - 1, 1) for t in bt]
        bt_l = [pltpu.roll(t, 1, 1) for t in bt]
        face = []
        for c in range(planes + 1):
            nxt = (c + 1) % (planes + 1)
            face.append(0.5 * (at[c] + jnp.where(lane == BS - 1, at_r[nxt], at_r[c])))
        face_l = [pltpu.roll(t, 1, 1) for t in face]
        here = row + sub
        row_ok = ((here >= TOP) | (me > 0)) & ((here < TOP + rows) | (me < ranks - 1))
        for c in range(planes + 1):
            nxt, prv = (c + 1) % (planes + 1), (c + planes) % (planes + 1)
            below = 0.5 * (at[c] + plane(a, a8, c, row + 1))
            above = 0.5 * (at[c] + plane(a, a8, c, row - 1))
            near_b = (
                plane(b, b8, c, row + 1)
                + plane(b, b8, c, row - 1)
                + jnp.where(lane == BS - 1, bt_r[nxt], bt_r[c])
                + jnp.where(lane == 0, bt_l[prv], bt_l[c])
            )
            diag = (
                16.0 * bt[c]
                + face[c]
                + jnp.where(lane == 0, face_l[prv], face_l[c])
                + below
                + above
                + near_b
            )
            ok = row_ok & side_ok if c == planes else row_ok
            fx[c, pl.ds(row, 8), :] = face[c]
            fy[c, pl.ds(row, 8), :] = below
            wt[c, pl.ds(row, 8), :] = jnp.where(ok, OMEGA / jnp.where(ok, diag, 1.0), 0.0)
        return carry

    lax.fori_loop(0, strips, step, 0)


def split3(x):
    high = x.astype(jnp.bfloat16)
    rest = x - high.astype(F32)
    mid = rest.astype(jnp.bfloat16)
    low = (rest - mid.astype(F32)).astype(jnp.bfloat16)
    return jnp.concatenate([high, mid, low], axis=1)


def refine_rows(src, put, strips):
    sub = subs()

    def step(k, carry):
        row = pl.multiple_of(8 * k, 8)
        x = src[pl.ds(row + 8, 8), :]
        up = src[pl.ds(row + 7, 8), :]
        down = src[pl.ds(row + 9, 8), :]
        part = lax.rem(k, 8)
        up = jnp.where((sub == 0) & (part == 1), x, up)
        down = jnp.where((sub == 7) & (part == 0), x, down)
        near = 0.75 * x
        put(row, near + 0.25 * up, near + 0.25 * down)
        return carry

    lax.fori_loop(0, strips, step, 0, unroll=2)


def refine_kernel(weights, left, middle, right, v, cols):
    gy_count = v.shape[0] // 2
    strips = left.shape[0] // 8
    for gy in range(gy_count):
        parent = left[...] if gy == 0 else right[...] if gy == gy_count - 1 else middle[gy - 1]
        wide = jnp.dot(split3(parent), weights[...], preferred_element_type=F32)
        for half in range(2):
            cols[gy, half, 8 : 8 + left.shape[0], :] = wide[:, half * BS : (half + 1) * BS]

            def put(row, even, odd, c=2 * gy + half):
                v[c, pl.ds(2 * row, 8, stride=2), :] = even
                v[c, pl.ds(2 * row + 1, 8, stride=2), :] = odd

            refine_rows(cols.at[gy, half], put, strips)


def sweep_kernel(weights, from_right, from_left, v, b, l, b8, l8, fx, fy, wt, out, v8, cols, m, h, v1):
    planes = v.shape[0]
    rows = out.shape[0]
    lane = lanes()
    cells = from_right.shape[0]
    wide_lane = lax.broadcasted_iota(jnp.int32, (cells, BS), 1)
    edge = jnp.where(wide_lane < BS // 2, from_right[...], from_left[...])
    cols[8 : 8 + cells, :] = jnp.dot(split3(edge), weights[...], preferred_element_type=F32)

    def put(row, even, odd):
        v8[pl.ds(2 * row, 8, stride=2), :] = even
        v8[pl.ds(2 * row + 1, 8, stride=2), :] = odd

    refine_rows(cols, put, cells // 8)

    def plane(ref, ref8, c, start):
        return ref8[pl.ds(start, 8), :] if c == planes else ref[c, pl.ds(start, 8), :]

    def right_of(ts):
        r = [pltpu.roll(t, BS - 1, 1) for t in ts]
        n = len(ts)
        return [jnp.where(lane == BS - 1, r[(c + 1) % n], r[c]) for c in range(n)]

    def left_of(ts):
        r = [pltpu.roll(t, 1, 1) for t in ts]
        n = len(ts)
        return [jnp.where(lane == 0, r[(c + n - 1) % n], r[c]) for c in range(n)]

    def moments(get):
        def step(k, carry):
            row = pl.multiple_of(TOP - 8 + 8 * k, 8)
            t = [get(c, row) for c in range(planes + 1)]
            dx = [r - x for r, x in zip(right_of(t), t)]
            q = [fx[c, pl.ds(row, 8), :] * dx[c] for c in range(planes + 1)]
            dxl, ql = left_of(dx), left_of(q)
            for c in range(planes + 1):
                dyd = get(c, row + 1) - t[c]
                dyu = t[c] - get(c, row - 1)
                lap = (dx[c] - dxl[c]) + (dyd - dyu)
                m[c, pl.ds(row, 8), :] = plane(b, b8, c, row) * lap
                div = (q[c] - ql[c]) + (
                    fy[c, pl.ds(row, 8), :] * dyd - fy[c, pl.ds(row - 1, 8), :] * dyu
                )
                h[c, pl.ds(row, 8), :] = plane(l, l8, c, row) + div
            return carry

        lax.fori_loop(0, rows // 8 + 2, step, 0, unroll=2)

    def update(first, count, get, put, width):
        def step(k, carry):
            row = pl.multiple_of(first + 8 * k, 8)
            t = [m[c, pl.ds(row, 8), :] for c in range(planes + 1)]
            tr, tl = right_of(t), left_of(t)
            for c in range(width):
                lap = (
                    tr[c] + tl[c] + m[c, pl.ds(row - 1, 8), :] + m[c, pl.ds(row + 1, 8), :]
                ) - 4.0 * t[c]
                put(c, row, get(c, row) + wt[c, pl.ds(row, 8), :] * (h[c, pl.ds(row, 8), :] - lap))
            return carry

        lax.fori_loop(0, count, step, 0, unroll=2)

    def start_value(c, row):
        return plane(v, v8, c, row)

    def put_middle(c, row, value):
        v1[c, pl.ds(row, 8), :] = value

    def middle_value(c, row):
        return v1[c, pl.ds(row, 8), :]

    def put_out(c, row, value):
        out[pl.ds(pl.multiple_of(row - TOP, 8), 8), c * BS : (c + 1) * BS] = value

    moments(start_value)
    update(TOP - 8, rows // 8 + 2, start_value, put_middle, planes + 1)
    moments(middle_value)
    update(TOP, rows // 8, middle_value, put_out, planes)


def quadrant_table(half_index):
    half_size = BS // 2
    row_ids = jnp.arange(BS, dtype=jnp.int32)[:, None]
    col_ids = jnp.arange(BS, dtype=jnp.int32)[None, :]
    base_cell = half_index * half_size
    near_cell = base_cell + row_ids // 2
    other_cell = near_cell + jnp.where(row_ids % 2 == 1, 1, -1)
    other_cell = jnp.clip(other_cell, base_cell, base_cell + half_size - 1)
    return 0.75 * (col_ids == near_cell).astype(F32) + 0.25 * (col_ids == other_cell).astype(F32)


def params(limit_mib):
    return pltpu.CompilerParams(vmem_limit_bytes=limit_mib << 20)


def shape(*dims):
    return jax.ShapeDtypeStruct(dims, F32)


def local(old_field, old_level, new_source, stretch_coef, bend_coef, load_field):
    per_device = old_field.shape[0]
    groups_x, groups_y = new_source.shape
    groups = groups_x * groups_y
    ranks, segments = lax.axis_size("wide"), lax.axis_size("narrow")
    dims = (ranks, groups, per_device, segments)
    rows, columns = load_field.shape
    planes = columns // BS
    tall = rows + 2 * TOP
    coarse = 2 * BS + 16
    up_links = [(i + 1, i) for i in range(ranks - 1)]
    down_links = [(i, i + 1) for i in range(ranks - 1)]
    left_links = [(i + 1, i) for i in range(segments - 1)]
    right_links = [(i, i + 1) for i in range(segments - 1)]

    facts = jnp.concatenate([new_source.reshape(-1), old_level])
    table = lax.all_to_all(
        jnp.broadcast_to(facts[None], (ranks, groups + per_device)), "wide", 0, 0, tiled=True
    )

    head = jnp.concatenate([stretch_coef[:3], bend_coef[:3], load_field[:2]])
    tail = jnp.concatenate([stretch_coef[-3:], bend_coef[-3:], load_field[-2:]])
    above = lax.ppermute(tail, "wide", down_links)
    below = lax.ppermute(head, "wide", up_links)

    table, above, below = lax.optimization_barrier((table, above, below))
    outgoing = pl.pallas_call(
        functools.partial(send_kernel, dims),
        out_shape=shape(ranks, coarse, BS),
        in_specs=[SMEM, VMEM],
        out_specs=HBM,
        scratch_shapes=[
            pltpu.VMEM((ranks, 16, BS), F32),
            pltpu.SemaphoreType.DMA((ranks, 2)),
            pltpu.SemaphoreType.DMA(()),
        ],
        compiler_params=params(8),
        name="send_build",
    )(table, old_field)
    incoming = lax.all_to_all(outgoing, "wide", 0, 0, tiled=True)

    a, b, l, to_left, to_right = pl.pallas_call(
        functools.partial(scale_kernel, dims),
        out_shape=[shape(planes, tall, BS)] * 3 + [shape(tall, BS)] * 2,
        in_specs=[SMEM] + [VMEM] * 5,
        out_specs=[VMEM] * 5,
        compiler_params=params(20),
        name="scale",
    )(table, stretch_coef, bend_coef, load_field, above, below)
    from_right = lax.ppermute(to_left, "narrow", left_links)
    from_left = lax.ppermute(to_right, "narrow", right_links)
    b8, l8, fx, fy, wt = pl.pallas_call(
        functools.partial(coef_kernel, dims),
        out_shape=[shape(tall, BS)] * 2 + [shape(planes + 1, tall, BS)] * 3,
        in_specs=[VMEM] * 5,
        out_specs=[VMEM] * 5,
        scratch_shapes=[pltpu.VMEM((tall, BS), F32)],
        compiler_params=params(24),
        name="coef",
    )(a, b, l, from_right, from_left)

    incoming, b8, l8, fx, fy, wt = lax.optimization_barrier((incoming, b8, l8, fx, fy, wt))

    left, middle, right = pl.pallas_call(
        functools.partial(take_kernel, dims),
        out_shape=[shape(coarse, BS), shape(groups_y - 2, coarse, BS), shape(coarse, BS)],
        in_specs=[SMEM, ANY],
        out_specs=[VMEM] * 3,
        scratch_shapes=[
            pltpu.VMEM((2 * groups_y, 8, BS), F32),
            pltpu.SemaphoreType.DMA((groups,)),
            pltpu.SemaphoreType.DMA((2 * groups_y,)),
        ],
        compiler_params=params(4),
        name="take",
    )(table, incoming)
    edge_right = lax.ppermute(left, "narrow", left_links)
    edge_left = lax.ppermute(right, "narrow", right_links)

    low, high = quadrant_table(0).T, quadrant_table(1).T
    both = jnp.concatenate([low, high], axis=1).astype(jnp.bfloat16)
    rim = jnp.concatenate([low[:, : BS // 2], high[:, BS // 2 :]], axis=1).astype(jnp.bfloat16)
    v = pl.pallas_call(
        refine_kernel,
        out_shape=shape(planes, tall, BS),
        in_specs=[VMEM] * 4,
        out_specs=VMEM,
        scratch_shapes=[pltpu.VMEM((groups_y, 2, coarse + 16, BS), F32)],
        compiler_params=params(12),
        name="refine",
    )(jnp.concatenate([both] * 3), left, middle, right)
    return pl.pallas_call(
        sweep_kernel,
        out_shape=shape(rows, columns),
        in_specs=[VMEM] * 11,
        out_specs=VMEM,
        scratch_shapes=[
            pltpu.VMEM((tall, BS), F32),
            pltpu.VMEM((coarse + 16, BS), F32),
            pltpu.VMEM((planes + 1, tall, BS), F32),
            pltpu.VMEM((planes + 1, tall, BS), F32),
            pltpu.VMEM((planes + 1, tall, BS), F32),
        ],
        compiler_params=params(32),
        name="sweeps",
    )(jnp.concatenate([rim] * 3), edge_right, edge_left, v, b, l, b8, l8, fx, fy, wt)


def solution(mesh):
    return jax.shard_map(
        local,
        mesh=mesh,
        in_specs=(
            P(("wide", "narrow"), None, None),
            P(("wide", "narrow")),
            P("wide", "narrow"),
            P("wide", "narrow"),
            P("wide", "narrow"),
            P("wide", "narrow"),
        ),
        out_specs=P("wide", "narrow"),
        check_vma=False,
    )
```

```python
import functools

import jax
import jax.numpy as jnp
import numpy as np
from jax import lax
from jax.experimental import pallas as pl
from jax.experimental.pallas import tpu as pltpu
from jax.sharding import PartitionSpec as P

OMEGA = 0.5
BS = 128
TOP = 16
BOTTOM = 24
F32 = jnp.float32
VMEM = pl.BlockSpec(memory_space=pltpu.VMEM)
SMEM = pl.BlockSpec(memory_space=pltpu.SMEM)
ANY = pl.BlockSpec(memory_space=pl.ANY)
HBM = pl.BlockSpec(memory_space=pltpu.HBM)


def lanes():
    return lax.broadcasted_iota(jnp.int32, (8, BS), 1)


def subs():
    return lax.broadcasted_iota(jnp.int32, (8, BS), 0)


def stage_kernel(a, b, l, head, tail, tiles, sems):
    rows = a.shape[0]
    copies = []
    for i, ref in enumerate((a, b, l)):
        copies.append(pltpu.make_async_copy(ref.at[0:8, :], tiles.at[i], sems.at[i]))
        copies.append(
            pltpu.make_async_copy(ref.at[rows - 8 : rows, :], tiles.at[3 + i], sems.at[3 + i])
        )
    for copy in copies:
        copy.start()
    for copy in copies:
        copy.wait()
    sub = lax.broadcasted_iota(jnp.int32, (8, a.shape[1]), 0)
    head[...] = jnp.where(
        sub < 3,
        tiles[0],
        jnp.where(sub < 6, pltpu.roll(tiles[1], 3, 0), pltpu.roll(tiles[2], 6, 0)),
    )
    tail[...] = jnp.where(
        sub < 3,
        pltpu.roll(tiles[3], 3, 0),
        jnp.where(sub < 6, pltpu.roll(tiles[4], 6, 0), tiles[5]),
    )


def rank_of(source, size):
    return source >> (size.bit_length() - 1) if size & (size - 1) == 0 else lax.div(source, size)


def rest_of(source, size):
    return source & (size - 1) if size & (size - 1) == 0 else lax.rem(source, size)


def source_of(table, groups, row, g):
    return table[row, g // (groups // 2), g % (groups // 2)]


def slot_of(owners, position):
    hit = jnp.int32(0)
    for earlier in range(position):
        hit = hit | (owners[earlier] == owners[position]).astype(jnp.int32)
    return hit


def send_kernel(dims, table, field, out, blocks, strip, in_sems, out_sems, strip_sem):
    ranks, groups, per_device, segments = dims
    me = lax.axis_index("wide")
    wanted = []

    def fetch(w, slot, local):
        return pltpu.make_async_copy(field.at[local], blocks.at[w, slot], in_sems.at[w, slot])

    def send(w, slot):
        return pltpu.make_async_copy(
            blocks.at[w, slot], out.at[w, pl.ds(slot * BS, BS), :], out_sems.at[w, slot]
        )

    for w in range(ranks):
        low, high, any_hit = jnp.int32(0), jnp.int32(0), jnp.int32(0)
        sources = [source_of(table, groups, w, g) for g in range(groups)]
        hits = [rank_of(source, per_device * segments) == me for source in sources]
        for source, hit in zip(sources, hits):
            high = jnp.where(hit, source, high)
            any_hit = jnp.where(hit, 1, any_hit)
        for source, hit in zip(reversed(sources), reversed(hits)):
            low = jnp.where(hit, source, low)
        low, high = rest_of(low, per_device), rest_of(high, per_device)
        wanted.append(any_hit)

        @pl.when(any_hit == 1)
        def _():
            fetch(w, 0, low).start()
            fetch(w, 1, high).start()

    for w in range(ranks):

        @pl.when(wanted[w] == 1)
        def _():
            for slot in range(2):
                fetch(w, slot, 0).wait()
                send(w, slot).start()

    sub = subs()
    for w in range(ranks):
        up, down = max(w - 1, 0), min(w + 1, ranks - 1)
        strip[w, 0:8, :] = jnp.where(
            sub < 4,
            pltpu.roll(blocks[up, 0, BS - 8 : BS, :], 4, 0),
            blocks[up, 1, BS - 8 : BS, :],
        )
        strip[w, 8:16, :] = jnp.where(
            sub < 4, blocks[down, 0, 0:8, :], pltpu.roll(blocks[down, 1, 0:8, :], 4, 0)
        )
    copy = pltpu.make_async_copy(strip, out.at[:, 2 * BS : 2 * BS + 16, :], strip_sem)
    copy.start()
    for w in range(ranks):

        @pl.when(wanted[w] == 1)
        def _():
            for slot in range(2):
                send(w, slot).wait()

    copy.wait()


def take_kernel(dims, table, recv, left, middle, right, tiles, sems, tile_sems):
    ranks, groups, per_device, segments = dims
    gy_count = groups // 2
    me = lax.axis_index("wide")
    up, down = jnp.maximum(me - 1, 0), jnp.minimum(me + 1, ranks - 1)

    def owners_of(row):
        return [
            rank_of(source_of(table, groups, row, g), per_device * segments) for g in range(groups)
        ]

    mine, above, below = owners_of(me), owners_of(up), owners_of(down)

    def column(gy):
        if gy == 0:
            return left
        if gy == gy_count - 1:
            return right
        return middle.at[gy - 1]

    copies = []
    for gx in range(2):
        for gy in range(gy_count):
            g = gx * gy_count + gy
            start = pl.multiple_of(slot_of(mine, g) * BS, BS)
            copies.append(
                pltpu.make_async_copy(
                    recv.at[mine[g], pl.ds(start, BS), :],
                    column(gy).at[8 + gx * BS : 8 + (gx + 1) * BS, :],
                    sems.at[g],
                )
            )
    for gy in range(gy_count):
        copies.append(
            pltpu.make_async_copy(
                recv.at[above[gy_count + gy], 2 * BS : 2 * BS + 8, :],
                tiles.at[gy],
                tile_sems.at[gy],
            )
        )
        copies.append(
            pltpu.make_async_copy(
                recv.at[below[gy], 2 * BS + 8 : 2 * BS + 16, :],
                tiles.at[gy_count + gy],
                tile_sems.at[gy_count + gy],
            )
        )
    for copy in copies:
        copy.start()
    for copy in copies:
        copy.wait()
    for gy in range(gy_count):
        tile = tiles[gy]
        tile = jnp.where(slot_of(above, gy_count + gy) == 0, pltpu.roll(tile, 4, 0), tile)
        column(gy)[0:8, :] = jnp.where(me > 0, tile, 0.0)
        tile = tiles[gy_count + gy]
        tile = jnp.where(slot_of(below, gy) == 1, pltpu.roll(tile, 4, 0), tile)
        column(gy)[8 + 2 * BS : 16 + 2 * BS, :] = jnp.where(me < ranks - 1, tile, 0.0)


def turn(x, by):
    return pltpu.roll(x, by % BS, 1)


def swap_stage(tiles, bit, lane):
    high = (lane & bit) != 0
    partner = lane ^ bit
    done = list(tiles)
    for low in range(len(tiles)):
        if not low & bit:
            first, second = tiles[low], tiles[low | bit]
            moved = jnp.take_along_axis(jnp.where(high, first, second), partner, axis=1)
            done[low] = jnp.where(high, moved, first)
            done[low | bit] = jnp.where(high, second, moved)
    return done


def interleave(tiles, lane):
    for bit in (1, 2):
        tiles = swap_stage(tiles, bit, lane)
    return tiles


def right_of(ts, lane):
    side = ts[-1]
    source = jnp.where(lane < BS - 4, lane + 4, jnp.where(lane == BS - 1, 0, lane - (BS - 5)))
    done = []
    for first in range(0, len(ts) - 1, 4):
        group = ts[first : first + 4]
        edge = jnp.where(lane == 0, ts[first + 4], group[0])
        done += group[1:] + [jnp.take_along_axis(edge, source, axis=1)]
    return done + [turn(jnp.where(lane == 0, ts[0], side), -1)]


def left_of(ts, lane):
    side = ts[-1]
    source = jnp.where(lane >= 4, lane - 4, jnp.where(lane == 0, BS - 1, lane + (BS - 5)))
    done = []
    for first in range(0, len(ts) - 1, 4):
        group = ts[first : first + 4]
        edge = jnp.where(lane == BS - 1, ts[first - 1], group[3])
        done += [jnp.take_along_axis(edge, source, axis=1)] + group[:3]
    return done + [turn(jnp.where(lane == BS - 1, ts[-2], side), 1)]


def spacing(dims, table, row, g):
    _, groups, per_device, segments = dims
    source = source_of(table, groups, row, g)
    level = table[rank_of(source, per_device * segments), 2, rest_of(source, per_device)]
    return jnp.where(level >= 1, F32(4.0), F32(1.0))


def halo_rows(dims, above, below, rows):
    me, ranks = lax.axis_index("wide"), dims[0]
    up, down = jnp.maximum(me - 1, 0), jnp.minimum(me + 1, ranks - 1)
    return (
        (TOP - 8, above, up, dims[1] // 2, (5, 2, 0)),
        (TOP + rows, below, down, 0, (0, 5, 2)),
    )


def pack_kernel(dims, table, a_in, b_in, l_in, above, below, to_left, to_right, raw, sems):
    rows, columns = a_in.shape
    gy_count = dims[1] // 2
    me = lax.axis_index("wide")
    copies = []
    for i, ref in enumerate((a_in, b_in, l_in)):
        for side, first in enumerate((0, columns - BS)):
            copies.append(
                pltpu.make_async_copy(
                    ref.at[:, first : first + BS], raw.at[side, i], sems.at[side, i]
                )
            )
    for copy in copies:
        copy.start()
    lane = lanes()

    def put_left(row, a, b, l):
        to_left[pl.ds(row, 8), :] = jnp.where(
            lane < 3, a, jnp.where(lane < 6, turn(b, 3), turn(l, 6))
        )

    def put_right(row, a, b, l):
        to_right[pl.ds(row, 8), :] = jnp.where(
            lane >= BS - 3, a, jnp.where(lane >= BS - 6, turn(b, -3), turn(l, -6))
        )

    for row, halo, base, at, turns in halo_rows(dims, above, below, rows):
        for put, first, gy in ((put_left, 0, 0), (put_right, columns - BS, gy_count - 1)):
            s = spacing(dims, table, base, at + gy)
            a, b, l = [pltpu.roll(halo[:, first : first + BS], by, 0) for by in turns]
            put(row, a * (0.5 * s), b * (s * s), l)
    for copy in copies:
        copy.wait()
    half = rows // 2
    for gx in range(2):
        s_left = spacing(dims, table, me, gx * gy_count)
        s_right = spacing(dims, table, me, gx * gy_count + gy_count - 1)

        def step(k, carry):
            row = pl.multiple_of(gx * half + 8 * k, 8)
            to = pl.multiple_of(row + TOP, 8)
            for side, put, s in ((0, put_left, s_left), (1, put_right, s_right)):
                a, b, l = [raw[side, i, pl.ds(row, 8), :] for i in range(3)]
                put(to, a * (0.5 * s), b * (s * s), l)
            return carry

        lax.fori_loop(0, half // 8, step, 0, unroll=4)


FX, FY, FYU, BEND, WEIGHT, LOAD = range(6)


def prep_kernel(
    dims, table, a_in, b_in, l_in, above, below, from_right, from_left, out, raw, a, k6, in_sems, out_sems
):
    ranks, groups, _, segments = dims
    gy_count = groups // 2
    planes = 2 * gy_count
    me, seg = lax.axis_index("wide"), lax.axis_index("narrow")
    rows = a_in.shape[0]
    chunks = in_sems.shape[1]
    size = rows // chunks
    lane, sub = lanes(), subs()
    strips = rows // 8 + 2
    near = lane < BS // 2
    cols = [slice(c * BS, (c + 1) * BS) for c in range(planes)]

    def read(i, chunk):
        ref = (a_in, b_in, l_in)[i]
        span = slice(chunk * size, (chunk + 1) * size)
        return pltpu.make_async_copy(ref.at[span, :], raw.at[i, span, :], in_sems.at[i, chunk])

    for chunk in range(chunks):
        for i in range(3):
            read(i, chunk).start()

    def side(k, carry):
        row = pl.multiple_of(TOP - 8 + 8 * k, 8)
        z = jnp.where(near, from_right[pl.ds(row, 8), :], from_left[pl.ds(row, 8), :])
        a[planes, pl.ds(row, 8), :] = z
        k6[BEND, planes, pl.ds(row, 8), :] = jnp.where(near, turn(z, -3), turn(z, 3))
        k6[LOAD, planes, pl.ds(row, 8), :] = jnp.where(near, turn(z, -6), turn(z, 6))
        return carry

    lax.fori_loop(0, strips, side, 0, unroll=6)

    def put(row, *arrays):
        for out_ref, tiles in zip((a, k6.at[BEND], k6.at[LOAD]), arrays):
            for c, tile in enumerate(interleave(tiles, lane)):
                out_ref[c, pl.ds(row, 8), :] = tile

    for row, halo, base, at, turns in halo_rows(dims, above, below, rows):
        s = [spacing(dims, table, base, at + gy) for gy in range(gy_count)]
        put(
            row,
            [pltpu.roll(halo[:, cols[c]], turns[0], 0) * (0.5 * s[c // 2]) for c in range(planes)],
            [pltpu.roll(halo[:, cols[c]], turns[1], 0) * (s[c // 2] * s[c // 2]) for c in range(planes)],
            [pltpu.roll(halo[:, cols[c]], turns[2], 0) for c in range(planes)],
        )
    for chunk in range(chunks):
        gx = 2 * chunk // chunks
        s = [spacing(dims, table, me, gx * gy_count + gy) for gy in range(gy_count)]
        for i in range(3):
            read(i, chunk).wait()

        def lay(k, carry):
            row = pl.multiple_of(chunk * size + k * 8, 8)
            put(
                pl.multiple_of(row + TOP, 8),
                [raw[0, pl.ds(row, 8), cols[c]] * (0.5 * s[c // 2]) for c in range(planes)],
                [raw[1, pl.ds(row, 8), cols[c]] * (s[c // 2] * s[c // 2]) for c in range(planes)],
                [raw[2, pl.ds(row, 8), cols[c]] for c in range(planes)],
            )
            return carry

        lax.fori_loop(0, size // 8, lay, 0, unroll=2)

    parts = out_sems.shape[1]
    part_size = strips // parts

    def write(i, part):
        span = slice(TOP - 8 + 8 * part * part_size, TOP - 8 + 8 * (part + 1) * part_size)
        return pltpu.make_async_copy(
            k6.at[i, :, span, :], out.at[i, :, span, :], out_sems.at[i, part]
        )

    for part in range(parts):
        for i in (BEND, LOAD):
            write(i, part).start()
    side_ok = ((lane < 2) & (seg < segments - 1)) | ((lane >= BS - 2) & (seg > 0))
    b = k6.at[BEND]

    def step(k, carry):
        row = pl.multiple_of(TOP - 8 + 8 * k, 8)
        at = [a[c, pl.ds(row, 8), :] for c in range(planes + 1)]
        bt = [b[c, pl.ds(row, 8), :] for c in range(planes + 1)]
        face = [x + y for x, y in zip(at, right_of(at, lane))]
        face_l = left_of(face, lane)
        bt_r, bt_l = right_of(bt, lane), left_of(bt, lane)
        here = row + sub
        row_ok = ((here >= TOP) | (me > 0)) & ((here < TOP + rows) | (me < ranks - 1))
        for c in range(planes + 1):
            below_face = at[c] + a[c, pl.ds(row + 1, 8), :]
            above_face = at[c] + a[c, pl.ds(row - 1, 8), :]
            near_b = b[c, pl.ds(row + 1, 8), :] + b[c, pl.ds(row - 1, 8), :] + bt_r[c] + bt_l[c]
            diag = 16.0 * bt[c] + face[c] + face_l[c] + below_face + above_face + near_b
            ok = row_ok & side_ok if c == planes else row_ok
            k6[FX, c, pl.ds(row, 8), :] = face[c]
            k6[FY, c, pl.ds(row, 8), :] = below_face
            k6[FYU, c, pl.ds(row, 8), :] = above_face
            k6[WEIGHT, c, pl.ds(row, 8), :] = jnp.where(ok, OMEGA / diag, 0.0)
        return carry

    for part in range(parts):
        lax.fori_loop(part * part_size, (part + 1) * part_size, step, 0, unroll=2)
        for i in (FX, FY, FYU, WEIGHT):
            write(i, part).start()
    for part in range(parts):
        for i in range(6):
            write(i, part).wait()


def split3(x):
    high = x.astype(jnp.bfloat16)
    rest = x - high.astype(F32)
    mid = rest.astype(jnp.bfloat16)
    low = (rest - mid.astype(F32)).astype(jnp.bfloat16)
    return jnp.concatenate([high, mid, low], axis=1)


def refine_rows(sources, put, strips):
    sub = subs()

    def step(k, carry):
        row = pl.multiple_of(8 * k, 8)
        part = lax.rem(k, 8)
        top, bottom = (sub == 0) & (part == 1), (sub == 7) & (part == 0)
        for c, src in enumerate(sources):
            x = src[pl.ds(row + 8, 8), :]
            up = jnp.where(top, x, src[pl.ds(row + 7, 8), :])
            down = jnp.where(bottom, x, src[pl.ds(row + 9, 8), :])
            near = 0.75 * x
            put(c, row, near + 0.25 * up, near + 0.25 * down)
        return carry

    lax.fori_loop(0, strips, step, 0, unroll=2)


def finish_kernel(
    group_weights, side_weights, left, middle, right, from_right, from_left, k_in,
    out, cols, edge, v, m, h, v1, k6, early_sems, late_sems,
):
    planes = cols.shape[0]
    gy_count = planes // 2
    coarse = left.shape[0]
    rows = out.shape[0]
    lane = lanes()
    chunks = early_sems.shape[1]
    strips = rows // 8 + 2
    size = strips // chunks

    def early(i, chunk):
        span = slice(TOP - 8 + 8 * chunk * size, TOP - 8 + 8 * (chunk + 1) * size)
        return pltpu.make_async_copy(
            k_in.at[i, :, span, :], k6.at[i, :, span, :], early_sems.at[i, chunk]
        )

    def late(i):
        span = slice(TOP - 8, TOP - 8 + 8 * strips)
        return pltpu.make_async_copy(
            k_in.at[i, :, span, :], k6.at[i, :, span, :], late_sems.at[i - WEIGHT]
        )

    for chunk in range(chunks):
        for i in (FX, FY, FYU, BEND):
            early(i, chunk).start()
    for i in (WEIGHT, LOAD):
        late(i).start()

    for gy in range(gy_count):
        parent = left[...] if gy == 0 else right[...] if gy == gy_count - 1 else middle[gy - 1]
        wide = jnp.dot(split3(parent), group_weights[...], preferred_element_type=F32)
        for half in range(2):
            cols[2 * gy + half, 8 : 8 + coarse, :] = wide[:, half * BS : (half + 1) * BS]
    wide_lane = lax.broadcasted_iota(jnp.int32, (coarse, BS), 1)
    beside = jnp.where(wide_lane < BS // 2, from_right[...], from_left[...])
    edge[8 : 8 + coarse, :] = jnp.dot(
        split3(beside), side_weights[...], preferred_element_type=F32
    )

    def mix(k, carry):
        row = pl.multiple_of(8 + 8 * k, 8)
        tiles = [cols[c, pl.ds(row, 8), :] for c in range(planes)]
        for c, tile in enumerate(swap_stage(tiles, 2, lane)):
            cols[c, pl.ds(row, 8), :] = tile
        return carry

    lax.fori_loop(0, coarse // 8, mix, 0, unroll=2)

    def put(c, row, even, odd):
        v[c, pl.ds(2 * row, 8, stride=2), :] = even
        v[c, pl.ds(2 * row + 1, 8, stride=2), :] = odd

    refine_rows([cols.at[c] for c in range(planes)] + [edge], put, coarse // 8)

    fx, fy, fyu, b, wt, l = [k6.at[i] for i in range(6)]

    def moments(u, waits):
        def step(k, carry):
            row = pl.multiple_of(TOP - 8 + 8 * k, 8)
            t = [u[c, pl.ds(row, 8), :] for c in range(planes + 1)]
            dx = [r - x for r, x in zip(right_of(t, lane), t)]
            q = [fx[c, pl.ds(row, 8), :] * dx[c] for c in range(planes + 1)]
            dxl, ql = left_of(dx, lane), left_of(q, lane)
            for c in range(planes + 1):
                dyd = u[c, pl.ds(row + 1, 8), :] - t[c]
                dyu = t[c] - u[c, pl.ds(row - 1, 8), :]
                lap = (dx[c] - dxl[c]) + (dyd - dyu)
                m[c, pl.ds(row, 8), :] = b[c, pl.ds(row, 8), :] * lap
                h[c, pl.ds(row, 8), :] = (q[c] - ql[c]) + (
                    fy[c, pl.ds(row, 8), :] * dyd - fyu[c, pl.ds(row, 8), :] * dyu
                )
            return carry

        for chunk in range(chunks if waits else 1):
            first, last = 0, strips
            if waits:
                first, last = chunk * size, (chunk + 1) * size
                for i in (FX, FY, FYU, BEND):
                    early(i, chunk).wait()
            lax.fori_loop(first, last, step, 0, unroll=2)

    def update(first, count, u, put, width, unroll):
        def step(k, carry):
            row = pl.multiple_of(first + 8 * k, 8)
            t = [m[c, pl.ds(row, 8), :] for c in range(planes + 1)]
            tr, tl = right_of(t, lane), left_of(t, lane)
            new = []
            for c in range(width):
                lap = (
                    tr[c] + tl[c] + m[c, pl.ds(row - 1, 8), :] + m[c, pl.ds(row + 1, 8), :]
                ) - 4.0 * t[c]
                rest = (l[c, pl.ds(row, 8), :] + h[c, pl.ds(row, 8), :]) - lap
                new.append(u[c, pl.ds(row, 8), :] + wt[c, pl.ds(row, 8), :] * rest)
            put(row, new)
            return carry

        lax.fori_loop(0, count, step, 0, unroll=unroll)

    def put_middle(row, new):
        for c, value in enumerate(new):
            v1[c, pl.ds(row, 8), :] = value

    def put_out(row, new):
        at = pl.multiple_of(row - TOP, 8)
        for c, value in enumerate(interleave(new, lane)):
            out[pl.ds(at, 8), c * BS : (c + 1) * BS] = value

    moments(v, True)
    for i in (WEIGHT, LOAD):
        late(i).wait()
    update(TOP - 8, strips, v, put_middle, planes + 1, 3)
    moments(v1, False)
    update(TOP, rows // 8, v1, put_out, planes, 4)


def quadrant_table(half_index):
    half_size = BS // 2
    row_ids, col_ids = np.arange(BS)[:, None], np.arange(BS)[None, :]
    base_cell = half_index * half_size
    near_cell = base_cell + row_ids // 2
    other_cell = near_cell + np.where(row_ids % 2 == 1, 1, -1)
    other_cell = np.clip(other_cell, base_cell, base_cell + half_size - 1)
    return 0.75 * (col_ids == near_cell) + 0.25 * (col_ids == other_cell)


def group_weights():
    low, high = quadrant_table(0).T, quadrant_table(1).T
    both = np.stack([low, high], axis=1).reshape(BS, 2, BS // 2, 2)
    both = both.transpose(0, 3, 2, 1).reshape(BS, 2 * BS)
    return jnp.asarray(np.concatenate([both] * 3), jnp.bfloat16)


def side_weights():
    low, high = quadrant_table(0).T, quadrant_table(1).T
    rim = np.where(np.arange(BS)[None, :] < BS // 2, low, high)
    return jnp.asarray(np.concatenate([rim] * 3), jnp.bfloat16)


def params(limit_mib):
    return pltpu.CompilerParams(vmem_limit_bytes=int(limit_mib * (1 << 20)))


def shape(*dims):
    return jax.ShapeDtypeStruct(dims, F32)


def local(old_field, old_level, new_source, stretch_coef, bend_coef, load_field):
    per_device = old_field.shape[0]
    groups_x, groups_y = new_source.shape
    groups = groups_x * groups_y
    ranks, segments = lax.axis_size("wide"), lax.axis_size("narrow")
    dims = (ranks, groups, per_device, segments)
    rows, columns = load_field.shape
    planes = columns // BS
    tall = rows + TOP + BOTTOM
    coarse = 2 * BS + 16
    up_links = [(i + 1, i) for i in range(ranks - 1)]
    down_links = [(i, i + 1) for i in range(ranks - 1)]
    left_links = [(i + 1, i) for i in range(segments - 1)]
    right_links = [(i, i + 1) for i in range(segments - 1)]

    facts = jnp.concatenate(
        [jnp.pad(new_source, ((0, 0), (0, per_device - groups_y))), old_level[None]]
    )
    table = lax.all_to_all(
        jnp.broadcast_to(facts[None], (ranks, *facts.shape)), "wide", 0, 0, tiled=True
    )

    head, tail = pl.pallas_call(
        stage_kernel,
        out_shape=[shape(8, columns), shape(8, columns)],
        in_specs=[HBM] * 3,
        out_specs=[VMEM] * 2,
        scratch_shapes=[pltpu.VMEM((6, 8, columns), F32), pltpu.SemaphoreType.DMA((6,))],
        compiler_params=params(62.3),
        name="stage_kernel",
    )(stretch_coef, bend_coef, load_field)
    above = lax.ppermute(tail, "wide", down_links)
    below = lax.ppermute(head, "wide", up_links)

    outgoing = pl.pallas_call(
        functools.partial(send_kernel, dims),
        out_shape=shape(ranks, coarse, BS),
        in_specs=[SMEM, HBM],
        out_specs=HBM,
        scratch_shapes=[
            pltpu.VMEM((ranks, 2, BS, BS), F32),
            pltpu.VMEM((ranks, 16, BS), F32),
            pltpu.SemaphoreType.DMA((ranks, 2)),
            pltpu.SemaphoreType.DMA((ranks, 2)),
            pltpu.SemaphoreType.DMA(()),
        ],
        compiler_params=params(62.3),
        name="send_build",
    )(table, old_field)
    incoming = lax.all_to_all(outgoing, "wide", 0, 0, tiled=True)

    to_left, to_right = pl.pallas_call(
        functools.partial(pack_kernel, dims),
        out_shape=[shape(tall, BS)] * 2,
        in_specs=[SMEM] + [HBM] * 3 + [VMEM] * 2,
        out_specs=[VMEM] * 2,
        scratch_shapes=[pltpu.VMEM((2, 3, rows, BS), F32), pltpu.SemaphoreType.DMA((2, 3))],
        compiler_params=params(62.3),
        name="pack",
    )(table, stretch_coef, bend_coef, load_field, above, below)
    from_right = lax.ppermute(to_left, "narrow", left_links)
    from_left = lax.ppermute(to_right, "narrow", right_links)
    coefs = pl.pallas_call(
        functools.partial(prep_kernel, dims),
        out_shape=shape(6, planes + 1, tall, BS),
        in_specs=[SMEM] + [HBM] * 3 + [VMEM] * 4,
        out_specs=HBM,
        scratch_shapes=[
            pltpu.VMEM((3, rows, columns), F32),
            pltpu.VMEM((planes + 1, tall, BS), F32),
            pltpu.VMEM((6, planes + 1, tall, BS), F32),
            pltpu.SemaphoreType.DMA((3, 4)),
            pltpu.SemaphoreType.DMA((6, 3)),
        ],
        compiler_params=params(62.3),
        name="prep_kernel",
    )(table, stretch_coef, bend_coef, load_field, above, below, from_right, from_left)

    left, middle, right = pl.pallas_call(
        functools.partial(take_kernel, dims),
        out_shape=[shape(coarse, BS), shape(groups_y - 2, coarse, BS), shape(coarse, BS)],
        in_specs=[SMEM, HBM],
        out_specs=[VMEM] * 3,
        scratch_shapes=[
            pltpu.VMEM((2 * groups_y, 8, BS), F32),
            pltpu.SemaphoreType.DMA((groups,)),
            pltpu.SemaphoreType.DMA((2 * groups_y,)),
        ],
        compiler_params=params(2),
        name="take",
    )(table, incoming)
    edge_right = lax.ppermute(left, "narrow", left_links)
    edge_left = lax.ppermute(right, "narrow", right_links)

    return pl.pallas_call(
        finish_kernel,
        out_shape=shape(rows, columns),
        in_specs=[VMEM] * 7 + [HBM],
        out_specs=VMEM,
        scratch_shapes=[
            pltpu.VMEM((planes, coarse + 16, BS), F32),
            pltpu.VMEM((coarse + 16, BS), F32),
        ]
        + [pltpu.VMEM((planes + 1, tall, BS), F32)] * 4
        + [
            pltpu.VMEM((6, planes + 1, tall, BS), F32),
            pltpu.SemaphoreType.DMA((4, 3)),
            pltpu.SemaphoreType.DMA((2,)),
        ],
        compiler_params=params(52),
        name="finish",
    )(group_weights(), side_weights(), left, middle, right, edge_right, edge_left, coefs)


def solution(mesh):
    return jax.shard_map(
        local,
        mesh=mesh,
        in_specs=(
            P(("wide", "narrow"), None, None),
            P(("wide", "narrow")),
            P("wide", "narrow"),
            P("wide", "narrow"),
            P("wide", "narrow"),
            P("wide", "narrow"),
        ),
        out_specs=P("wide", "narrow"),
        check_vma=False,
    )
```

```python
import functools

import jax
import jax.numpy as jnp
import numpy as np
from jax import lax
from jax.experimental import pallas as pl
from jax.experimental.pallas import tpu as pltpu
from jax.sharding import PartitionSpec as P

OMEGA = 0.5
BS = 128
TOP = 16
BOTTOM = 24
F32 = jnp.float32
VMEM = pl.BlockSpec(memory_space=pltpu.VMEM)
SMEM = pl.BlockSpec(memory_space=pltpu.SMEM)
ANY = pl.BlockSpec(memory_space=pl.ANY)
HBM = pl.BlockSpec(memory_space=pltpu.HBM)


def lanes():
    return lax.broadcasted_iota(jnp.int32, (8, BS), 1)


def subs():
    return lax.broadcasted_iota(jnp.int32, (8, BS), 0)


def stage_kernel(a, b, l, head, tail, tiles, sems):
    rows = a.shape[0]
    copies = []
    for i, ref in enumerate((a, b, l)):
        copies.append(pltpu.make_async_copy(ref.at[0:8, :], tiles.at[i], sems.at[i]))
        copies.append(
            pltpu.make_async_copy(ref.at[rows - 8 : rows, :], tiles.at[3 + i], sems.at[3 + i])
        )
    for copy in copies:
        copy.start()
    for copy in copies:
        copy.wait()
    sub = lax.broadcasted_iota(jnp.int32, (8, a.shape[1]), 0)
    head[...] = jnp.where(
        sub < 3,
        tiles[0],
        jnp.where(sub < 6, pltpu.roll(tiles[1], 3, 0), pltpu.roll(tiles[2], 6, 0)),
    )
    tail[...] = jnp.where(
        sub < 3,
        pltpu.roll(tiles[3], 3, 0),
        jnp.where(sub < 6, pltpu.roll(tiles[4], 6, 0), tiles[5]),
    )


def rank_of(source, size):
    return source >> (size.bit_length() - 1) if size & (size - 1) == 0 else lax.div(source, size)


def rest_of(source, size):
    return source & (size - 1) if size & (size - 1) == 0 else lax.rem(source, size)


def source_of(table, groups, row, g):
    return table[row, g // (groups // 2), g % (groups // 2)]


def slot_of(owners, position):
    hit = jnp.int32(0)
    for earlier in range(position):
        hit = hit | (owners[earlier] == owners[position]).astype(jnp.int32)
    return hit


def send_kernel(dims, table, field, out, strip, sems, strip_sem):
    ranks, groups, per_device, segments = dims
    me = lax.axis_index("wide")
    picked, wanted = [], []

    def send(w, slot, local):
        return pltpu.make_async_copy(
            field.at[local], out.at[w, pl.ds(slot * BS, BS), :], sems.at[w, slot]
        )

    for w in range(ranks):
        low, high, any_hit = jnp.int32(0), jnp.int32(0), jnp.int32(0)
        sources = [source_of(table, groups, w, g) for g in range(groups)]
        hits = [rank_of(source, per_device * segments) == me for source in sources]
        for source, hit in zip(sources, hits):
            high = jnp.where(hit, source, high)
            any_hit = jnp.where(hit, 1, any_hit)
        for source, hit in zip(reversed(sources), reversed(hits)):
            low = jnp.where(hit, source, low)
        low, high = rest_of(low, per_device), rest_of(high, per_device)
        picked.append((low, high))
        wanted.append(any_hit)

        @pl.when(any_hit == 1)
        def _():
            send(w, 0, low).start()
            send(w, 1, high).start()

    sub = subs()
    for w in range(ranks):
        up, down = picked[max(w - 1, 0)], picked[min(w + 1, ranks - 1)]
        strip[w, 0:8, :] = jnp.where(
            sub < 4,
            pltpu.roll(field[up[0], BS - 8 : BS, :], 4, 0),
            field[up[1], BS - 8 : BS, :],
        )
        strip[w, 8:16, :] = jnp.where(
            sub < 4, field[down[0], 0:8, :], pltpu.roll(field[down[1], 0:8, :], 4, 0)
        )
    copy = pltpu.make_async_copy(strip, out.at[:, 2 * BS : 2 * BS + 16, :], strip_sem)
    copy.start()
    for w in range(ranks):

        @pl.when(wanted[w] == 1)
        def _():
            for slot in range(2):
                send(w, slot, 0).wait()

    copy.wait()


def take_kernel(dims, table, recv, left, middle, right, tiles, sems, tile_sems):
    ranks, groups, per_device, segments = dims
    gy_count = groups // 2
    me = lax.axis_index("wide")
    up, down = jnp.maximum(me - 1, 0), jnp.minimum(me + 1, ranks - 1)

    def owners_of(row):
        return [
            rank_of(source_of(table, groups, row, g), per_device * segments) for g in range(groups)
        ]

    mine, above, below = owners_of(me), owners_of(up), owners_of(down)

    def column(gy):
        if gy == 0:
            return left
        if gy == gy_count - 1:
            return right
        return middle.at[gy - 1]

    copies = []
    for gx in range(2):
        for gy in range(gy_count):
            g = gx * gy_count + gy
            start = pl.multiple_of(slot_of(mine, g) * BS, BS)
            copies.append(
                pltpu.make_async_copy(
                    recv.at[mine[g], pl.ds(start, BS), :],
                    column(gy).at[8 + gx * BS : 8 + (gx + 1) * BS, :],
                    sems.at[g],
                )
            )
    for gy in range(gy_count):
        copies.append(
            pltpu.make_async_copy(
                recv.at[above[gy_count + gy], 2 * BS : 2 * BS + 8, :],
                tiles.at[gy],
                tile_sems.at[gy],
            )
        )
        copies.append(
            pltpu.make_async_copy(
                recv.at[below[gy], 2 * BS + 8 : 2 * BS + 16, :],
                tiles.at[gy_count + gy],
                tile_sems.at[gy_count + gy],
            )
        )
    for copy in copies:
        copy.start()
    for copy in copies:
        copy.wait()
    for gy in range(gy_count):
        tile = tiles[gy]
        tile = jnp.where(slot_of(above, gy_count + gy) == 0, pltpu.roll(tile, 4, 0), tile)
        column(gy)[0:8, :] = jnp.where(me > 0, tile, 0.0)
        tile = tiles[gy_count + gy]
        tile = jnp.where(slot_of(below, gy) == 1, pltpu.roll(tile, 4, 0), tile)
        column(gy)[8 + 2 * BS : 16 + 2 * BS, :] = jnp.where(me < ranks - 1, tile, 0.0)


def turn(x, by):
    return pltpu.roll(x, by % BS, 1)


def swap_stage(tiles, bit, lane):
    high = (lane & bit) != 0
    partner = lane ^ bit
    done = list(tiles)
    for low in range(len(tiles)):
        if not low & bit:
            first, second = tiles[low], tiles[low | bit]
            moved = jnp.take_along_axis(jnp.where(high, first, second), partner, axis=1)
            done[low] = jnp.where(high, moved, first)
            done[low | bit] = jnp.where(high, second, moved)
    return done


def interleave(tiles, lane):
    for bit in (1, 2):
        tiles = swap_stage(tiles, bit, lane)
    return tiles


def right_of(ts, lane):
    side = ts[-1]
    source = jnp.where(lane < BS - 4, lane + 4, jnp.where(lane == BS - 1, 0, lane - (BS - 5)))
    done = []
    for first in range(0, len(ts) - 1, 4):
        group = ts[first : first + 4]
        edge = jnp.where(lane == 0, ts[first + 4], group[0])
        done += group[1:] + [jnp.take_along_axis(edge, source, axis=1)]
    return done + [turn(jnp.where(lane == 0, ts[0], side), -1)]


def left_of(ts, lane):
    side = ts[-1]
    source = jnp.where(lane >= 4, lane - 4, jnp.where(lane == 0, BS - 1, lane + (BS - 5)))
    done = []
    for first in range(0, len(ts) - 1, 4):
        group = ts[first : first + 4]
        edge = jnp.where(lane == BS - 1, ts[first - 1], group[3])
        done += [jnp.take_along_axis(edge, source, axis=1)] + group[:3]
    return done + [turn(jnp.where(lane == BS - 1, ts[-2], side), 1)]


def spacing(dims, table, row, g):
    _, groups, per_device, segments = dims
    source = source_of(table, groups, row, g)
    level = table[rank_of(source, per_device * segments), 2, rest_of(source, per_device)]
    return jnp.where(level >= 1, F32(4.0), F32(1.0))


def halo_rows(dims, above, below, rows):
    me, ranks = lax.axis_index("wide"), dims[0]
    up, down = jnp.maximum(me - 1, 0), jnp.minimum(me + 1, ranks - 1)
    return (
        (TOP - 8, above, up, dims[1] // 2, (5, 2, 0)),
        (TOP + rows, below, down, 0, (0, 5, 2)),
    )


def pack_kernel(dims, table, a_in, b_in, l_in, above, below, to_left, to_right, raw, sems):
    rows, columns = a_in.shape
    gy_count = dims[1] // 2
    me = lax.axis_index("wide")
    copies = []
    for i, ref in enumerate((a_in, b_in, l_in)):
        for side, first in enumerate((0, columns - BS)):
            copies.append(
                pltpu.make_async_copy(
                    ref.at[:, first : first + BS], raw.at[side, i], sems.at[side, i]
                )
            )
    for copy in copies:
        copy.start()
    lane = lanes()
    strips = rows // 8 + 2
    per_tile = BS // 8
    halos = halo_rows(dims, above, below, rows)

    def strip_of(k, side):
        gy = side * (gy_count - 1)
        first = side * (columns - BS)
        if 0 < k < strips - 1:
            s = own[2 * (k - 1) // (strips - 2)][side]
            a, b, l = [raw[side, i, 8 * (k - 1) : 8 * k, :] for i in range(3)]
        else:
            _, halo, base, at, turns = halos[0 if k == 0 else 1]
            s = spacing(dims, table, base, at + gy)
            a, b, l = [pltpu.roll(halo[:, first : first + BS], by, 0) for by in turns]
        return a * (0.5 * s), b * (s * s), l

    own = [
        [spacing(dims, table, me, gx * gy_count + side * (gy_count - 1)) for side in range(2)]
        for gx in range(2)
    ]
    for copy in copies:
        copy.wait()
    for side, out in ((0, to_left), (1, to_right)):
        sign = 1 - 2 * side
        for tile in range(out.shape[0] // 8):
            packed = jnp.zeros((8, BS), F32)
            for slot in range(per_tile):
                k = tile * per_tile + slot
                if k >= strips:
                    break
                place = (lane - 8 * slot) & (BS - 1)
                place = place if side == 0 else BS - 1 - place
                a, b, l = strip_of(k, side)
                packed = jnp.where(place < 3, turn(a, 8 * slot), packed)
                packed = jnp.where((place >= 3) & (place < 6), turn(b, 8 * slot + 3 * sign), packed)
                packed = jnp.where((place >= 6) & (place < 8), turn(l, 8 * slot + 6 * sign), packed)
            out[8 * tile : 8 * tile + 8, :] = packed


FX, FY, FYU, BEND, WEIGHT, LOAD = range(6)


def prep_kernel(
    dims, table, a_in, b_in, l_in, above, below, from_right, from_left, out, raw, a, k6, in_sems, out_sems
):
    ranks, groups, _, segments = dims
    gy_count = groups // 2
    planes = 2 * gy_count
    me, seg = lax.axis_index("wide"), lax.axis_index("narrow")
    rows = a_in.shape[0]
    chunks = in_sems.shape[1]
    size = rows // chunks
    lane, sub = lanes(), subs()
    strips = rows // 8 + 2
    near = lane < BS // 2
    cols = [slice(c * BS, (c + 1) * BS) for c in range(planes)]

    def read(i, chunk):
        ref = (a_in, b_in, l_in)[i]
        span = slice(chunk * size, (chunk + 1) * size)
        return pltpu.make_async_copy(ref.at[span, :], raw.at[i, span, :], in_sems.at[i, chunk])

    for chunk in range(chunks):
        for i in range(3):
            read(i, chunk).start()

    per_tile = BS // 8
    for k in range(strips):
        tile, slot = k // per_tile, k % per_tile
        at = slice(8 * tile, 8 * tile + 8)
        z = jnp.where(((lane - 8 * slot) & (BS - 1)) < 8, from_right[at, :], from_left[at, :])
        here = slice(TOP - 8 + 8 * k, TOP + 8 * k)
        a[planes, here, :] = turn(z, -8 * slot)
        k6[BEND, planes, here, :] = jnp.where(
            near, turn(z, -8 * slot - 3), turn(z, -8 * slot + 3)
        )
        k6[LOAD, planes, here, :] = jnp.where(
            near, turn(z, -8 * slot - 6), turn(z, -8 * slot + 6)
        )

    def put(row, *arrays):
        for out_ref, tiles in zip((a, k6.at[BEND], k6.at[LOAD]), arrays):
            for c, tile in enumerate(interleave(tiles, lane)):
                out_ref[c, pl.ds(row, 8), :] = tile

    for row, halo, base, at, turns in halo_rows(dims, above, below, rows):
        s = [spacing(dims, table, base, at + gy) for gy in range(gy_count)]
        put(
            row,
            [pltpu.roll(halo[:, cols[c]], turns[0], 0) * (0.5 * s[c // 2]) for c in range(planes)],
            [pltpu.roll(halo[:, cols[c]], turns[1], 0) * (s[c // 2] * s[c // 2]) for c in range(planes)],
            [pltpu.roll(halo[:, cols[c]], turns[2], 0) for c in range(planes)],
        )
    for chunk in range(chunks):
        gx = 2 * chunk // chunks
        s = [spacing(dims, table, me, gx * gy_count + gy) for gy in range(gy_count)]
        for i in range(3):
            read(i, chunk).wait()

        def lay(k, carry):
            row = pl.multiple_of(chunk * size + k * 8, 8)
            put(
                pl.multiple_of(row + TOP, 8),
                [raw[0, pl.ds(row, 8), cols[c]] * (0.5 * s[c // 2]) for c in range(planes)],
                [raw[1, pl.ds(row, 8), cols[c]] * (s[c // 2] * s[c // 2]) for c in range(planes)],
                [raw[2, pl.ds(row, 8), cols[c]] for c in range(planes)],
            )
            return carry

        lax.fori_loop(0, size // 8, lay, 0, unroll=4)

    parts = out_sems.shape[1]
    part_size = strips // parts

    def write(i, part):
        span = slice(TOP - 8 + 8 * part * part_size, TOP - 8 + 8 * (part + 1) * part_size)
        return pltpu.make_async_copy(
            k6.at[i, :, span, :], out.at[i, :, span, :], out_sems.at[i, part]
        )

    for part in range(parts):
        for i in (BEND, LOAD):
            write(i, part).start()
    side_ok = ((lane < 2) & (seg < segments - 1)) | ((lane >= BS - 2) & (seg > 0))
    b = k6.at[BEND]

    def step(k, carry):
        row = pl.multiple_of(TOP - 8 + 8 * k, 8)
        at = [a[c, pl.ds(row, 8), :] for c in range(planes + 1)]
        bt = [b[c, pl.ds(row, 8), :] for c in range(planes + 1)]
        face = [x + y for x, y in zip(at, right_of(at, lane))]
        face_l = left_of(face, lane)
        bt_r, bt_l = right_of(bt, lane), left_of(bt, lane)
        here = row + sub
        row_ok = ((here >= TOP) | (me > 0)) & ((here < TOP + rows) | (me < ranks - 1))
        for c in range(planes + 1):
            below_face = at[c] + a[c, pl.ds(row + 1, 8), :]
            above_face = at[c] + a[c, pl.ds(row - 1, 8), :]
            near_b = b[c, pl.ds(row + 1, 8), :] + b[c, pl.ds(row - 1, 8), :] + bt_r[c] + bt_l[c]
            diag = 16.0 * bt[c] + face[c] + face_l[c] + below_face + above_face + near_b
            ok = row_ok & side_ok if c == planes else row_ok
            k6[FX, c, pl.ds(row, 8), :] = face[c]
            k6[FY, c, pl.ds(row, 8), :] = below_face
            k6[FYU, c, pl.ds(row, 8), :] = above_face
            k6[WEIGHT, c, pl.ds(row, 8), :] = jnp.where(ok, OMEGA / diag, 0.0)
        return carry

    for part in range(parts):
        lax.fori_loop(part * part_size, (part + 1) * part_size, step, 0, unroll=11)
        for i in (FX, FY, FYU, WEIGHT):
            write(i, part).start()
    for part in range(parts):
        for i in range(6):
            write(i, part).wait()


def split3(x):
    high = x.astype(jnp.bfloat16)
    rest = x - high.astype(F32)
    mid = rest.astype(jnp.bfloat16)
    low = (rest - mid.astype(F32)).astype(jnp.bfloat16)
    return jnp.concatenate([high, mid, low], axis=1)


def refine_rows(sources, put, strips):
    sub = subs()

    def step(k, carry):
        row = pl.multiple_of(8 * k, 8)
        part = lax.rem(k, 8)
        top, bottom = (sub == 0) & (part == 1), (sub == 7) & (part == 0)
        for c, src in enumerate(sources):
            x = src[pl.ds(row + 8, 8), :]
            up = jnp.where(top, x, src[pl.ds(row + 7, 8), :])
            down = jnp.where(bottom, x, src[pl.ds(row + 9, 8), :])
            near = 0.75 * x
            put(c, row, near + 0.25 * up, near + 0.25 * down)
        return carry

    lax.fori_loop(0, strips, step, 0, unroll=2)


def finish_kernel(
    group_weights, side_weights, left, middle, right, from_right, from_left, k_in,
    out, cols, edge, v, m, h, v1, k6, early_sems, late_sems,
):
    planes = cols.shape[0]
    gy_count = planes // 2
    coarse = left.shape[0]
    rows = out.shape[0]
    lane = lanes()
    chunks = early_sems.shape[1]
    strips = rows // 8 + 2
    size = strips // chunks

    def early(i, chunk):
        span = slice(TOP - 8 + 8 * chunk * size, TOP - 8 + 8 * (chunk + 1) * size)
        return pltpu.make_async_copy(
            k_in.at[i, :, span, :], k6.at[i, :, span, :], early_sems.at[i, chunk]
        )

    def late(i):
        span = slice(TOP - 8, TOP - 8 + 8 * strips)
        return pltpu.make_async_copy(
            k_in.at[i, :, span, :], k6.at[i, :, span, :], late_sems.at[i - WEIGHT]
        )

    for chunk in range(chunks):
        for i in (FX, FY, FYU, BEND):
            early(i, chunk).start()
    for i in (WEIGHT, LOAD):
        late(i).start()

    for gy in range(gy_count):
        parent = left[...] if gy == 0 else right[...] if gy == gy_count - 1 else middle[gy - 1]
        wide = jnp.dot(split3(parent), group_weights[...], preferred_element_type=F32)
        for half in range(2):
            cols[2 * gy + half, 8 : 8 + coarse, :] = wide[:, half * BS : (half + 1) * BS]
    wide_lane = lax.broadcasted_iota(jnp.int32, (coarse, BS), 1)
    beside = jnp.where(wide_lane < BS // 2, from_right[...], from_left[...])
    edge[8 : 8 + coarse, :] = jnp.dot(
        split3(beside), side_weights[...], preferred_element_type=F32
    )

    def mix(k, carry):
        row = pl.multiple_of(8 + 8 * k, 8)
        tiles = [cols[c, pl.ds(row, 8), :] for c in range(planes)]
        for c, tile in enumerate(swap_stage(tiles, 2, lane)):
            cols[c, pl.ds(row, 8), :] = tile
        return carry

    lax.fori_loop(0, coarse // 8, mix, 0, unroll=2)

    def put(c, row, even, odd):
        v[c, pl.ds(2 * row, 8, stride=2), :] = even
        v[c, pl.ds(2 * row + 1, 8, stride=2), :] = odd

    refine_rows([cols.at[c] for c in range(planes)] + [edge], put, coarse // 8)

    fx, fy, fyu, b, wt, l = [k6.at[i] for i in range(6)]

    def moments(u, waits):
        def step(k, carry):
            row = pl.multiple_of(TOP - 8 + 8 * k, 8)
            t = [u[c, pl.ds(row, 8), :] for c in range(planes + 1)]
            dx = [r - x for r, x in zip(right_of(t, lane), t)]
            q = [fx[c, pl.ds(row, 8), :] * dx[c] for c in range(planes + 1)]
            dxl, ql = left_of(dx, lane), left_of(q, lane)
            for c in range(planes + 1):
                dyd = u[c, pl.ds(row + 1, 8), :] - t[c]
                dyu = t[c] - u[c, pl.ds(row - 1, 8), :]
                lap = (dx[c] - dxl[c]) + (dyd - dyu)
                m[c, pl.ds(row, 8), :] = b[c, pl.ds(row, 8), :] * lap
                h[c, pl.ds(row, 8), :] = (q[c] - ql[c]) + (
                    fy[c, pl.ds(row, 8), :] * dyd - fyu[c, pl.ds(row, 8), :] * dyu
                )
            return carry

        for chunk in range(chunks if waits else 1):
            first, last = 0, strips
            if waits:
                first, last = chunk * size, (chunk + 1) * size
                for i in (FX, FY, FYU, BEND):
                    early(i, chunk).wait()
            lax.fori_loop(first, last, step, 0, unroll=11)

    def update(first, count, u, put, width, unroll):
        def step(k, carry):
            row = pl.multiple_of(first + 8 * k, 8)
            t = [m[c, pl.ds(row, 8), :] for c in range(planes + 1)]
            tr, tl = right_of(t, lane), left_of(t, lane)
            new = []
            for c in range(width):
                lap = (
                    tr[c] + tl[c] + m[c, pl.ds(row - 1, 8), :] + m[c, pl.ds(row + 1, 8), :]
                ) - 4.0 * t[c]
                rest = (l[c, pl.ds(row, 8), :] + h[c, pl.ds(row, 8), :]) - lap
                new.append(u[c, pl.ds(row, 8), :] + wt[c, pl.ds(row, 8), :] * rest)
            put(row, new)
            return carry

        lax.fori_loop(0, count, step, 0, unroll=unroll)

    def put_middle(row, new):
        for c, value in enumerate(new):
            v1[c, pl.ds(row, 8), :] = value

    def put_out(row, new):
        at = pl.multiple_of(row - TOP, 8)
        for c, value in enumerate(interleave(new, lane)):
            out[pl.ds(at, 8), c * BS : (c + 1) * BS] = value

    moments(v, True)
    for i in (WEIGHT, LOAD):
        late(i).wait()
    update(TOP - 8, strips, v, put_middle, planes + 1, 11)
    moments(v1, False)
    update(TOP, rows // 8, v1, put_out, planes, 8)


def quadrant_table(half_index):
    half_size = BS // 2
    row_ids, col_ids = np.arange(BS)[:, None], np.arange(BS)[None, :]
    base_cell = half_index * half_size
    near_cell = base_cell + row_ids // 2
    other_cell = near_cell + np.where(row_ids % 2 == 1, 1, -1)
    other_cell = np.clip(other_cell, base_cell, base_cell + half_size - 1)
    return 0.75 * (col_ids == near_cell) + 0.25 * (col_ids == other_cell)


def group_weights():
    low, high = quadrant_table(0).T, quadrant_table(1).T
    both = np.stack([low, high], axis=1).reshape(BS, 2, BS // 2, 2)
    both = both.transpose(0, 3, 2, 1).reshape(BS, 2 * BS)
    return jnp.asarray(np.concatenate([both] * 3), jnp.bfloat16)


def side_weights():
    low, high = quadrant_table(0).T, quadrant_table(1).T
    rim = np.where(np.arange(BS)[None, :] < BS // 2, low, high)
    return jnp.asarray(np.concatenate([rim] * 3), jnp.bfloat16)


def params(limit_mib):
    return pltpu.CompilerParams(vmem_limit_bytes=int(limit_mib * (1 << 20)))


def shape(*dims):
    return jax.ShapeDtypeStruct(dims, F32)


def local(old_field, old_level, new_source, stretch_coef, bend_coef, load_field):
    per_device = old_field.shape[0]
    groups_x, groups_y = new_source.shape
    groups = groups_x * groups_y
    ranks, segments = lax.axis_size("wide"), lax.axis_size("narrow")
    dims = (ranks, groups, per_device, segments)
    rows, columns = load_field.shape
    planes = columns // BS
    tall = rows + TOP + BOTTOM
    coarse = 2 * BS + 16
    packet = 8 * -(-(rows // 8 + 2) // (BS // 8))
    up_links = [(i + 1, i) for i in range(ranks - 1)]
    down_links = [(i, i + 1) for i in range(ranks - 1)]
    left_links = [(i + 1, i) for i in range(segments - 1)]
    right_links = [(i, i + 1) for i in range(segments - 1)]

    facts = jnp.concatenate(
        [jnp.pad(new_source, ((0, 0), (0, per_device - groups_y))), old_level[None]]
    )
    table = lax.all_to_all(
        jnp.broadcast_to(facts[None], (ranks, *facts.shape)), "wide", 0, 0, tiled=True
    )

    head, tail = pl.pallas_call(
        stage_kernel,
        out_shape=[shape(8, columns), shape(8, columns)],
        in_specs=[HBM] * 3,
        out_specs=[VMEM] * 2,
        scratch_shapes=[pltpu.VMEM((6, 8, columns), F32), pltpu.SemaphoreType.DMA((6,))],
        compiler_params=params(62.3),
        name="stage_kernel",
    )(stretch_coef, bend_coef, load_field)
    above = lax.ppermute(tail, "wide", down_links)
    below = lax.ppermute(head, "wide", up_links)

    outgoing = pl.pallas_call(
        functools.partial(send_kernel, dims),
        out_shape=shape(ranks, coarse, BS),
        in_specs=[SMEM, VMEM],
        out_specs=HBM,
        scratch_shapes=[
            pltpu.VMEM((ranks, 16, BS), F32),
            pltpu.SemaphoreType.DMA((ranks, 2)),
            pltpu.SemaphoreType.DMA(()),
        ],
        compiler_params=params(62.3),
        name="send_build",
    )(table, old_field)
    incoming = lax.all_to_all(outgoing, "wide", 0, 0, tiled=True)

    to_left, to_right = pl.pallas_call(
        functools.partial(pack_kernel, dims),
        out_shape=[shape(packet, BS)] * 2,
        in_specs=[SMEM] + [HBM] * 3 + [VMEM] * 2,
        out_specs=[VMEM] * 2,
        scratch_shapes=[pltpu.VMEM((2, 3, rows, BS), F32), pltpu.SemaphoreType.DMA((2, 3))],
        compiler_params=params(62.3),
        name="pack",
    )(table, stretch_coef, bend_coef, load_field, above, below)
    from_right = lax.ppermute(to_left, "narrow", left_links)
    from_left = lax.ppermute(to_right, "narrow", right_links)
    coefs = pl.pallas_call(
        functools.partial(prep_kernel, dims),
        out_shape=shape(6, planes + 1, tall, BS),
        in_specs=[SMEM] + [HBM] * 3 + [VMEM] * 4,
        out_specs=HBM,
        scratch_shapes=[
            pltpu.VMEM((3, rows, columns), F32),
            pltpu.VMEM((planes + 1, tall, BS), F32),
            pltpu.VMEM((6, planes + 1, tall, BS), F32),
            pltpu.SemaphoreType.DMA((3, 4)),
            pltpu.SemaphoreType.DMA((6, 3)),
        ],
        compiler_params=params(62.3),
        name="prep_kernel",
    )(table, stretch_coef, bend_coef, load_field, above, below, from_right, from_left)

    left, middle, right = pl.pallas_call(
        functools.partial(take_kernel, dims),
        out_shape=[shape(coarse, BS), shape(groups_y - 2, coarse, BS), shape(coarse, BS)],
        in_specs=[SMEM, HBM],
        out_specs=[VMEM] * 3,
        scratch_shapes=[
            pltpu.VMEM((2 * groups_y, 8, BS), F32),
            pltpu.SemaphoreType.DMA((groups,)),
            pltpu.SemaphoreType.DMA((2 * groups_y,)),
        ],
        compiler_params=params(2),
        name="take",
    )(table, incoming)
    edge_right = lax.ppermute(left, "narrow", left_links)
    edge_left = lax.ppermute(right, "narrow", right_links)

    return pl.pallas_call(
        finish_kernel,
        out_shape=shape(rows, columns),
        in_specs=[VMEM] * 7 + [HBM],
        out_specs=VMEM,
        scratch_shapes=[
            pltpu.VMEM((planes, coarse + 16, BS), F32),
            pltpu.VMEM((coarse + 16, BS), F32),
        ]
        + [pltpu.VMEM((planes + 1, tall, BS), F32)] * 4
        + [
            pltpu.VMEM((6, planes + 1, tall, BS), F32),
            pltpu.SemaphoreType.DMA((4, 2)),
            pltpu.SemaphoreType.DMA((2,)),
        ],
        compiler_params=params(52),
        name="finish",
    )(group_weights(), side_weights(), left, middle, right, edge_right, edge_left, coefs)


def solution(mesh):
    return jax.shard_map(
        local,
        mesh=mesh,
        in_specs=(
            P(("wide", "narrow"), None, None),
            P(("wide", "narrow")),
            P("wide", "narrow"),
            P("wide", "narrow"),
            P("wide", "narrow"),
            P("wide", "narrow"),
        ),
        out_specs=P("wide", "narrow"),
        check_vma=False,
    )
```

```python
import functools

import jax
import jax.numpy as jnp
import numpy as np
from jax import lax
from jax.experimental import pallas as pl
from jax.experimental.pallas import tpu as pltpu
from jax.sharding import PartitionSpec as P

OMEGA = 0.5
BS = 128
TOP = 16
BOTTOM = 24
F32 = jnp.float32
VMEM = pl.BlockSpec(memory_space=pltpu.VMEM)
SMEM = pl.BlockSpec(memory_space=pltpu.SMEM)
ANY = pl.BlockSpec(memory_space=pl.ANY)
HBM = pl.BlockSpec(memory_space=pltpu.HBM)


def lanes():
    return lax.broadcasted_iota(jnp.int32, (8, BS), 1)


def subs():
    return lax.broadcasted_iota(jnp.int32, (8, BS), 0)


def stage_kernel(a, b, l, head, tail, tiles, sems):
    rows = a.shape[0]
    copies = []
    for i, ref in enumerate((a, b, l)):
        copies.append(pltpu.make_async_copy(ref.at[0:8, :], tiles.at[i], sems.at[i]))
        copies.append(
            pltpu.make_async_copy(ref.at[rows - 8 : rows, :], tiles.at[3 + i], sems.at[3 + i])
        )
    for copy in copies:
        copy.start()
    for copy in copies:
        copy.wait()
    sub = lax.broadcasted_iota(jnp.int32, (8, a.shape[1]), 0)
    head[...] = jnp.where(
        sub < 3,
        tiles[0],
        jnp.where(sub < 6, pltpu.roll(tiles[1], 3, 0), pltpu.roll(tiles[2], 6, 0)),
    )
    tail[...] = jnp.where(
        sub < 3,
        pltpu.roll(tiles[3], 3, 0),
        jnp.where(sub < 6, pltpu.roll(tiles[4], 6, 0), tiles[5]),
    )


def rank_of(source, size):
    return source >> (size.bit_length() - 1) if size & (size - 1) == 0 else lax.div(source, size)


def rest_of(source, size):
    return source & (size - 1) if size & (size - 1) == 0 else lax.rem(source, size)


def source_of(table, groups, row, g):
    return table[row, g // (groups // 2), g % (groups // 2)]


def slot_of(owners, position):
    hit = jnp.int32(0)
    for earlier in range(position):
        hit = hit | (owners[earlier] == owners[position]).astype(jnp.int32)
    return hit


def send_kernel(dims, table, field, out, strip, sems, strip_sem):
    ranks, groups, per_device, segments = dims
    me = lax.axis_index("wide")
    picked, wanted = [], []

    def send(w, slot, local):
        return pltpu.make_async_copy(
            field.at[local], out.at[w, pl.ds(slot * BS, BS), :], sems.at[w, slot]
        )

    for w in range(ranks):
        low, high, any_hit = jnp.int32(0), jnp.int32(0), jnp.int32(0)
        sources = [source_of(table, groups, w, g) for g in range(groups)]
        hits = [rank_of(source, per_device * segments) == me for source in sources]
        for source, hit in zip(sources, hits):
            high = jnp.where(hit, source, high)
            any_hit = jnp.where(hit, 1, any_hit)
        for source, hit in zip(reversed(sources), reversed(hits)):
            low = jnp.where(hit, source, low)
        low, high = rest_of(low, per_device), rest_of(high, per_device)
        picked.append((low, high))
        wanted.append(any_hit)

        @pl.when(any_hit == 1)
        def _():
            send(w, 0, low).start()
            send(w, 1, high).start()

    sub = subs()
    for w in range(ranks):
        up, down = picked[max(w - 1, 0)], picked[min(w + 1, ranks - 1)]
        strip[w, 0:8, :] = jnp.where(
            sub < 4,
            pltpu.roll(field[up[0], BS - 8 : BS, :], 4, 0),
            field[up[1], BS - 8 : BS, :],
        )
        strip[w, 8:16, :] = jnp.where(
            sub < 4, field[down[0], 0:8, :], pltpu.roll(field[down[1], 0:8, :], 4, 0)
        )
    copy = pltpu.make_async_copy(strip, out.at[:, 2 * BS : 2 * BS + 16, :], strip_sem)
    copy.start()
    for w in range(ranks):

        @pl.when(wanted[w] == 1)
        def _():
            for slot in range(2):
                send(w, slot, 0).wait()

    copy.wait()


def take_kernel(dims, table, recv, left, middle, right, tiles, sems, tile_sems):
    ranks, groups, per_device, segments = dims
    gy_count = groups // 2
    me = lax.axis_index("wide")
    up, down = jnp.maximum(me - 1, 0), jnp.minimum(me + 1, ranks - 1)

    def owners_of(row):
        return [
            rank_of(source_of(table, groups, row, g), per_device * segments) for g in range(groups)
        ]

    mine, above, below = owners_of(me), owners_of(up), owners_of(down)

    def column(gy):
        if gy == 0:
            return left
        if gy == gy_count - 1:
            return right
        return middle.at[gy - 1]

    copies = []
    for gx in range(2):
        for gy in range(gy_count):
            g = gx * gy_count + gy
            start = pl.multiple_of(slot_of(mine, g) * BS, BS)
            copies.append(
                pltpu.make_async_copy(
                    recv.at[mine[g], pl.ds(start, BS), :],
                    column(gy).at[8 + gx * BS : 8 + (gx + 1) * BS, :],
                    sems.at[g],
                )
            )
    for gy in range(gy_count):
        copies.append(
            pltpu.make_async_copy(
                recv.at[above[gy_count + gy], 2 * BS : 2 * BS + 8, :],
                tiles.at[gy],
                tile_sems.at[gy],
            )
        )
        copies.append(
            pltpu.make_async_copy(
                recv.at[below[gy], 2 * BS + 8 : 2 * BS + 16, :],
                tiles.at[gy_count + gy],
                tile_sems.at[gy_count + gy],
            )
        )
    for copy in copies:
        copy.start()
    for copy in copies:
        copy.wait()
    for gy in range(gy_count):
        tile = tiles[gy]
        tile = jnp.where(slot_of(above, gy_count + gy) == 0, pltpu.roll(tile, 4, 0), tile)
        column(gy)[0:8, :] = jnp.where(me > 0, tile, 0.0)
        tile = tiles[gy_count + gy]
        tile = jnp.where(slot_of(below, gy) == 1, pltpu.roll(tile, 4, 0), tile)
        column(gy)[8 + 2 * BS : 16 + 2 * BS, :] = jnp.where(me < ranks - 1, tile, 0.0)


def turn(x, by):
    return pltpu.roll(x, by % BS, 1)


def swap_stage(tiles, bit, lane):
    high = (lane & bit) != 0
    partner = lane ^ bit
    done = list(tiles)
    for low in range(len(tiles)):
        if not low & bit:
            first, second = tiles[low], tiles[low | bit]
            moved = jnp.take_along_axis(jnp.where(high, first, second), partner, axis=1)
            done[low] = jnp.where(high, moved, first)
            done[low | bit] = jnp.where(high, second, moved)
    return done


def interleave(tiles, lane):
    for bit in (1, 2):
        tiles = swap_stage(tiles, bit, lane)
    return tiles


def right_of(ts, lane):
    side = ts[-1]
    source = jnp.where(lane < BS - 4, lane + 4, jnp.where(lane == BS - 1, 0, lane - (BS - 5)))
    done = []
    for first in range(0, len(ts) - 1, 4):
        group = ts[first : first + 4]
        edge = jnp.where(lane == 0, ts[first + 4], group[0])
        done += group[1:] + [jnp.take_along_axis(edge, source, axis=1)]
    return done + [turn(jnp.where(lane == 0, ts[0], side), -1)]


def left_of(ts, lane):
    side = ts[-1]
    source = jnp.where(lane >= 4, lane - 4, jnp.where(lane == 0, BS - 1, lane + (BS - 5)))
    done = []
    for first in range(0, len(ts) - 1, 4):
        group = ts[first : first + 4]
        edge = jnp.where(lane == BS - 1, ts[first - 1], group[3])
        done += [jnp.take_along_axis(edge, source, axis=1)] + group[:3]
    return done + [turn(jnp.where(lane == BS - 1, ts[-2], side), 1)]


def spacing(dims, table, row, g):
    _, groups, per_device, segments = dims
    source = source_of(table, groups, row, g)
    level = table[rank_of(source, per_device * segments), 2, rest_of(source, per_device)]
    return jnp.where(level >= 1, F32(4.0), F32(1.0))


def halo_rows(dims, above, below, rows):
    me, ranks = lax.axis_index("wide"), dims[0]
    up, down = jnp.maximum(me - 1, 0), jnp.minimum(me + 1, ranks - 1)
    return (
        (TOP - 8, above, up, dims[1] // 2, (5, 2, 0)),
        (TOP + rows, below, down, 0, (0, 5, 2)),
    )


def pack_kernel(dims, table, a_in, b_in, l_in, above, below, to_left, to_right, raw, sems):
    rows, columns = a_in.shape
    gy_count = dims[1] // 2
    me = lax.axis_index("wide")
    copies = []
    for i, ref in enumerate((a_in, b_in, l_in)):
        for side, first in enumerate((0, columns - BS)):
            copies.append(
                pltpu.make_async_copy(
                    ref.at[:, first : first + BS], raw.at[side, i], sems.at[side, i]
                )
            )
    for copy in copies:
        copy.start()
    lane = lanes()
    strips = rows // 8 + 2
    per_tile = BS // 8
    halos = halo_rows(dims, above, below, rows)

    def strip_of(k, side):
        gy = side * (gy_count - 1)
        first = side * (columns - BS)
        if 0 < k < strips - 1:
            s = own[2 * (k - 1) // (strips - 2)][side]
            a, b, l = [raw[side, i, 8 * (k - 1) : 8 * k, :] for i in range(3)]
        else:
            _, halo, base, at, turns = halos[0 if k == 0 else 1]
            s = spacing(dims, table, base, at + gy)
            a, b, l = [pltpu.roll(halo[:, first : first + BS], by, 0) for by in turns]
        return a * (0.5 * s), b * (s * s), l

    own = [
        [spacing(dims, table, me, gx * gy_count + side * (gy_count - 1)) for side in range(2)]
        for gx in range(2)
    ]
    for copy in copies:
        copy.wait()
    for side, out in ((0, to_left), (1, to_right)):
        sign = 1 - 2 * side
        for tile in range(out.shape[0] // 8):
            packed = jnp.zeros((8, BS), F32)
            for slot in range(per_tile):
                k = tile * per_tile + slot
                if k >= strips:
                    break
                place = (lane - 8 * slot) & (BS - 1)
                place = place if side == 0 else BS - 1 - place
                a, b, l = strip_of(k, side)
                packed = jnp.where(place < 3, turn(a, 8 * slot), packed)
                packed = jnp.where((place >= 3) & (place < 6), turn(b, 8 * slot + 3 * sign), packed)
                packed = jnp.where((place >= 6) & (place < 8), turn(l, 8 * slot + 6 * sign), packed)
            out[8 * tile : 8 * tile + 8, :] = packed


FX, FY, BEND, WEIGHT, LOAD = range(5)


def prep_kernel(
    dims, table, a_in, b_in, l_in, above, below, from_right, from_left, out, raw, a, kept, in_sems, out_sems
):
    ranks, groups, _, segments = dims
    gy_count = groups // 2
    planes = 2 * gy_count
    me, seg = lax.axis_index("wide"), lax.axis_index("narrow")
    rows = a_in.shape[0]
    chunks = in_sems.shape[1]
    size = rows // chunks
    lane, sub = lanes(), subs()
    strips = rows // 8 + 2
    near = lane < BS // 2
    cols = [slice(c * BS, (c + 1) * BS) for c in range(planes)]

    def read(i, chunk):
        ref = (a_in, b_in, l_in)[i]
        span = slice(chunk * size, (chunk + 1) * size)
        return pltpu.make_async_copy(ref.at[span, :], raw.at[i, span, :], in_sems.at[i, chunk])

    for chunk in range(chunks):
        for i in range(3):
            read(i, chunk).start()

    per_tile = BS // 8
    for k in range(strips):
        tile, slot = k // per_tile, k % per_tile
        at = slice(8 * tile, 8 * tile + 8)
        z = jnp.where(((lane - 8 * slot) & (BS - 1)) < 8, from_right[at, :], from_left[at, :])
        here = slice(TOP - 8 + 8 * k, TOP + 8 * k)
        a[planes, here, :] = turn(z, -8 * slot)
        kept[BEND, planes, here, :] = jnp.where(
            near, turn(z, -8 * slot - 3), turn(z, -8 * slot + 3)
        )
        kept[LOAD, planes, here, :] = jnp.where(
            near, turn(z, -8 * slot - 6), turn(z, -8 * slot + 6)
        )

    def put(row, *arrays):
        for out_ref, tiles in zip((a, kept.at[BEND], kept.at[LOAD]), arrays):
            for c, tile in enumerate(interleave(tiles, lane)):
                out_ref[c, pl.ds(row, 8), :] = tile

    for row, halo, base, at, turns in halo_rows(dims, above, below, rows):
        s = [spacing(dims, table, base, at + gy) for gy in range(gy_count)]
        put(
            row,
            [pltpu.roll(halo[:, cols[c]], turns[0], 0) * (0.5 * s[c // 2]) for c in range(planes)],
            [pltpu.roll(halo[:, cols[c]], turns[1], 0) * (s[c // 2] * s[c // 2]) for c in range(planes)],
            [pltpu.roll(halo[:, cols[c]], turns[2], 0) for c in range(planes)],
        )
    for chunk in range(chunks):
        gx = 2 * chunk // chunks
        s = [spacing(dims, table, me, gx * gy_count + gy) for gy in range(gy_count)]
        for i in range(3):
            read(i, chunk).wait()

        def lay(k, carry):
            row = pl.multiple_of(chunk * size + k * 8, 8)
            put(
                pl.multiple_of(row + TOP, 8),
                [raw[0, pl.ds(row, 8), cols[c]] * (0.5 * s[c // 2]) for c in range(planes)],
                [raw[1, pl.ds(row, 8), cols[c]] * (s[c // 2] * s[c // 2]) for c in range(planes)],
                [raw[2, pl.ds(row, 8), cols[c]] for c in range(planes)],
            )
            return carry

        lax.fori_loop(0, size // 8, lay, 0, unroll=4)

    parts = out_sems.shape[1]
    part_size = strips // parts

    def write(i, part):
        span = slice(TOP - 8 + 8 * part * part_size, TOP - 8 + 8 * (part + 1) * part_size)
        return pltpu.make_async_copy(
            kept.at[i, :, span, :], out.at[i, :, span, :], out_sems.at[i, part]
        )

    for part in range(parts):
        for i in (BEND, LOAD):
            write(i, part).start()
    side_ok = ((lane < 2) & (seg < segments - 1)) | ((lane >= BS - 2) & (seg > 0))
    b = kept.at[BEND]

    def step(k, carry):
        row = pl.multiple_of(TOP - 8 + 8 * k, 8)
        at = [a[c, pl.ds(row, 8), :] for c in range(planes + 1)]
        bt = [b[c, pl.ds(row, 8), :] for c in range(planes + 1)]
        face = [x + y for x, y in zip(at, right_of(at, lane))]
        face_l = left_of(face, lane)
        bt_r, bt_l = right_of(bt, lane), left_of(bt, lane)
        here = row + sub
        row_ok = ((here >= TOP) | (me > 0)) & ((here < TOP + rows) | (me < ranks - 1))
        for c in range(planes + 1):
            below_face = at[c] + a[c, pl.ds(row + 1, 8), :]
            above_face = at[c] + a[c, pl.ds(row - 1, 8), :]
            near_b = b[c, pl.ds(row + 1, 8), :] + b[c, pl.ds(row - 1, 8), :] + bt_r[c] + bt_l[c]
            diag = 16.0 * bt[c] + face[c] + face_l[c] + below_face + above_face + near_b
            ok = row_ok & side_ok if c == planes else row_ok
            kept[FX, c, pl.ds(row, 8), :] = face[c]
            kept[FY, c, pl.ds(row, 8), :] = below_face
            kept[WEIGHT, c, pl.ds(row, 8), :] = jnp.where(ok, OMEGA / diag, 0.0)
        return carry

    for part in range(parts):
        lax.fori_loop(part * part_size, (part + 1) * part_size, step, 0, unroll=11)
        for i in (FX, FY, WEIGHT):
            write(i, part).start()
    for part in range(parts):
        for i in range(5):
            write(i, part).wait()


def split3(x):
    high = x.astype(jnp.bfloat16)
    rest = x - high.astype(F32)
    mid = rest.astype(jnp.bfloat16)
    low = (rest - mid.astype(F32)).astype(jnp.bfloat16)
    return jnp.concatenate([high, mid, low], axis=1)


def refine_rows(sources, put, strips):
    sub = subs()

    def step(k, carry):
        row = pl.multiple_of(8 * k, 8)
        part = lax.rem(k, 8)
        top, bottom = (sub == 0) & (part == 1), (sub == 7) & (part == 0)
        for c, src in enumerate(sources):
            x = src[pl.ds(row + 8, 8), :]
            up = jnp.where(top, x, src[pl.ds(row + 7, 8), :])
            down = jnp.where(bottom, x, src[pl.ds(row + 9, 8), :])
            near = 0.75 * x
            put(c, row, near + 0.25 * up, near + 0.25 * down)
        return carry

    lax.fori_loop(0, strips, step, 0, unroll=2)


def finish_kernel(
    group_weights, side_weights, left, middle, right, from_right, from_left, k_in,
    out, cols, edge, v, m, h, v1, kept, early_sems, late_sems,
):
    planes = cols.shape[0]
    gy_count = planes // 2
    coarse = left.shape[0]
    rows = out.shape[0]
    lane = lanes()
    chunks = early_sems.shape[1]
    strips = rows // 8 + 2
    size = strips // chunks

    def early(i, chunk):
        span = slice(TOP - 8 + 8 * chunk * size, TOP - 8 + 8 * (chunk + 1) * size)
        return pltpu.make_async_copy(
            k_in.at[i, :, span, :], kept.at[i, :, span, :], early_sems.at[i, chunk]
        )

    def late(i):
        span = slice(TOP - 8, TOP - 8 + 8 * strips)
        return pltpu.make_async_copy(
            k_in.at[i, :, span, :], kept.at[i, :, span, :], late_sems.at[i - WEIGHT]
        )

    for chunk in range(chunks):
        for i in (FX, FY, BEND):
            early(i, chunk).start()
    for i in (WEIGHT, LOAD):
        late(i).start()

    for gy in range(gy_count):
        parent = left[...] if gy == 0 else right[...] if gy == gy_count - 1 else middle[gy - 1]
        wide = jnp.dot(split3(parent), group_weights[...], preferred_element_type=F32)
        for half in range(2):
            cols[2 * gy + half, 8 : 8 + coarse, :] = wide[:, half * BS : (half + 1) * BS]
    wide_lane = lax.broadcasted_iota(jnp.int32, (coarse, BS), 1)
    beside = jnp.where(wide_lane < BS // 2, from_right[...], from_left[...])
    edge[8 : 8 + coarse, :] = jnp.dot(
        split3(beside), side_weights[...], preferred_element_type=F32
    )

    def mix(k, carry):
        row = pl.multiple_of(8 + 8 * k, 8)
        tiles = [cols[c, pl.ds(row, 8), :] for c in range(planes)]
        for c, tile in enumerate(swap_stage(tiles, 2, lane)):
            cols[c, pl.ds(row, 8), :] = tile
        return carry

    lax.fori_loop(0, coarse // 8, mix, 0, unroll=2)

    def put(c, row, even, odd):
        v[c, pl.ds(2 * row, 8, stride=2), :] = even
        v[c, pl.ds(2 * row + 1, 8, stride=2), :] = odd

    refine_rows([cols.at[c] for c in range(planes)] + [edge], put, coarse // 8)

    fx, fy, b, wt, l = [kept.at[i] for i in range(5)]

    def moments(u, waits):
        def step(k, carry):
            row = pl.multiple_of(TOP - 8 + 8 * k, 8)
            t = [u[c, pl.ds(row, 8), :] for c in range(planes + 1)]
            dx = [r - x for r, x in zip(right_of(t, lane), t)]
            q = [fx[c, pl.ds(row, 8), :] * dx[c] for c in range(planes + 1)]
            dxl, ql = left_of(dx, lane), left_of(q, lane)
            for c in range(planes + 1):
                dyd = u[c, pl.ds(row + 1, 8), :] - t[c]
                dyu = t[c] - u[c, pl.ds(row - 1, 8), :]
                lap = (dx[c] - dxl[c]) + (dyd - dyu)
                m[c, pl.ds(row, 8), :] = b[c, pl.ds(row, 8), :] * lap
                h[c, pl.ds(row, 8), :] = (q[c] - ql[c]) + (
                    fy[c, pl.ds(row, 8), :] * dyd - fy[c, pl.ds(row - 1, 8), :] * dyu
                )
            return carry

        for chunk in range(chunks if waits else 1):
            first, last = 0, strips
            if waits:
                first, last = chunk * size, (chunk + 1) * size
                for i in (FX, FY, BEND):
                    early(i, chunk).wait()
            lax.fori_loop(first, last, step, 0, unroll=11)

    def update(first, count, u, put, width, unroll):
        def step(k, carry):
            row = pl.multiple_of(first + 8 * k, 8)
            t = [m[c, pl.ds(row, 8), :] for c in range(planes + 1)]
            tr, tl = right_of(t, lane), left_of(t, lane)
            new = []
            for c in range(width):
                lap = (
                    tr[c] + tl[c] + m[c, pl.ds(row - 1, 8), :] + m[c, pl.ds(row + 1, 8), :]
                ) - 4.0 * t[c]
                rest = (l[c, pl.ds(row, 8), :] + h[c, pl.ds(row, 8), :]) - lap
                new.append(u[c, pl.ds(row, 8), :] + wt[c, pl.ds(row, 8), :] * rest)
            put(row, new)
            return carry

        lax.fori_loop(0, count, step, 0, unroll=unroll)

    def put_middle(row, new):
        for c, value in enumerate(new):
            v1[c, pl.ds(row, 8), :] = value

    def put_out(row, new):
        at = pl.multiple_of(row - TOP, 8)
        for c, value in enumerate(interleave(new, lane)):
            out[pl.ds(at, 8), c * BS : (c + 1) * BS] = value

    moments(v, True)
    for i in (WEIGHT, LOAD):
        late(i).wait()
    update(TOP - 8, strips, v, put_middle, planes + 1, 11)
    moments(v1, False)
    update(TOP, rows // 8, v1, put_out, planes, 8)


def quadrant_table(half_index):
    half_size = BS // 2
    row_ids, col_ids = np.arange(BS)[:, None], np.arange(BS)[None, :]
    base_cell = half_index * half_size
    near_cell = base_cell + row_ids // 2
    other_cell = near_cell + np.where(row_ids % 2 == 1, 1, -1)
    other_cell = np.clip(other_cell, base_cell, base_cell + half_size - 1)
    return 0.75 * (col_ids == near_cell) + 0.25 * (col_ids == other_cell)


def group_weights():
    low, high = quadrant_table(0).T, quadrant_table(1).T
    both = np.stack([low, high], axis=1).reshape(BS, 2, BS // 2, 2)
    both = both.transpose(0, 3, 2, 1).reshape(BS, 2 * BS)
    return jnp.asarray(np.concatenate([both] * 3), jnp.bfloat16)


def side_weights():
    low, high = quadrant_table(0).T, quadrant_table(1).T
    rim = np.where(np.arange(BS)[None, :] < BS // 2, low, high)
    return jnp.asarray(np.concatenate([rim] * 3), jnp.bfloat16)


def params(limit_mib):
    return pltpu.CompilerParams(vmem_limit_bytes=int(limit_mib * (1 << 20)))


def shape(*dims):
    return jax.ShapeDtypeStruct(dims, F32)


def local(old_field, old_level, new_source, stretch_coef, bend_coef, load_field):
    per_device = old_field.shape[0]
    groups_x, groups_y = new_source.shape
    groups = groups_x * groups_y
    ranks, segments = lax.axis_size("wide"), lax.axis_size("narrow")
    dims = (ranks, groups, per_device, segments)
    rows, columns = load_field.shape
    planes = columns // BS
    tall = rows + TOP + BOTTOM
    coarse = 2 * BS + 16
    packet = 8 * -(-(rows // 8 + 2) // (BS // 8))
    up_links = [(i + 1, i) for i in range(ranks - 1)]
    down_links = [(i, i + 1) for i in range(ranks - 1)]
    left_links = [(i + 1, i) for i in range(segments - 1)]
    right_links = [(i, i + 1) for i in range(segments - 1)]

    facts = jnp.concatenate(
        [jnp.pad(new_source, ((0, 0), (0, per_device - groups_y))), old_level[None]]
    )
    table = lax.all_to_all(
        jnp.broadcast_to(facts[None], (ranks, *facts.shape)), "wide", 0, 0, tiled=True
    )

    head, tail = pl.pallas_call(
        stage_kernel,
        out_shape=[shape(8, columns), shape(8, columns)],
        in_specs=[HBM] * 3,
        out_specs=[VMEM] * 2,
        scratch_shapes=[pltpu.VMEM((6, 8, columns), F32), pltpu.SemaphoreType.DMA((6,))],
        compiler_params=params(62.3),
        name="stage_kernel",
    )(stretch_coef, bend_coef, load_field)
    above = lax.ppermute(tail, "wide", down_links)
    below = lax.ppermute(head, "wide", up_links)

    outgoing = pl.pallas_call(
        functools.partial(send_kernel, dims),
        out_shape=shape(ranks, coarse, BS),
        in_specs=[SMEM, VMEM],
        out_specs=HBM,
        scratch_shapes=[
            pltpu.VMEM((ranks, 16, BS), F32),
            pltpu.SemaphoreType.DMA((ranks, 2)),
            pltpu.SemaphoreType.DMA(()),
        ],
        compiler_params=params(62.3),
        name="send_build",
    )(table, old_field)
    incoming = lax.all_to_all(outgoing, "wide", 0, 0, tiled=True)

    to_left, to_right = pl.pallas_call(
        functools.partial(pack_kernel, dims),
        out_shape=[shape(packet, BS)] * 2,
        in_specs=[SMEM] + [HBM] * 3 + [VMEM] * 2,
        out_specs=[VMEM] * 2,
        scratch_shapes=[pltpu.VMEM((2, 3, rows, BS), F32), pltpu.SemaphoreType.DMA((2, 3))],
        compiler_params=params(62.3),
        name="pack",
    )(table, stretch_coef, bend_coef, load_field, above, below)
    from_right = lax.ppermute(to_left, "narrow", left_links)
    from_left = lax.ppermute(to_right, "narrow", right_links)
    coefs = pl.pallas_call(
        functools.partial(prep_kernel, dims),
        out_shape=shape(5, planes + 1, tall, BS),
        in_specs=[SMEM] + [HBM] * 3 + [VMEM] * 4,
        out_specs=HBM,
        scratch_shapes=[
            pltpu.VMEM((3, rows, columns), F32),
            pltpu.VMEM((planes + 1, tall, BS), F32),
            pltpu.VMEM((5, planes + 1, tall, BS), F32),
            pltpu.SemaphoreType.DMA((3, 4)),
            pltpu.SemaphoreType.DMA((5, 3)),
        ],
        compiler_params=params(62.3),
        name="prep_kernel",
    )(table, stretch_coef, bend_coef, load_field, above, below, from_right, from_left)

    left, middle, right = pl.pallas_call(
        functools.partial(take_kernel, dims),
        out_shape=[shape(coarse, BS), shape(groups_y - 2, coarse, BS), shape(coarse, BS)],
        in_specs=[SMEM, HBM],
        out_specs=[VMEM] * 3,
        scratch_shapes=[
            pltpu.VMEM((2 * groups_y, 8, BS), F32),
            pltpu.SemaphoreType.DMA((groups,)),
            pltpu.SemaphoreType.DMA((2 * groups_y,)),
        ],
        compiler_params=params(2),
        name="take",
    )(table, incoming)
    edge_right = lax.ppermute(left, "narrow", left_links)
    edge_left = lax.ppermute(right, "narrow", right_links)

    return pl.pallas_call(
        finish_kernel,
        out_shape=shape(rows, columns),
        in_specs=[VMEM] * 7 + [HBM],
        out_specs=VMEM,
        scratch_shapes=[
            pltpu.VMEM((planes, coarse + 16, BS), F32),
            pltpu.VMEM((coarse + 16, BS), F32),
        ]
        + [pltpu.VMEM((planes + 1, tall, BS), F32)] * 4
        + [
            pltpu.VMEM((5, planes + 1, tall, BS), F32),
            pltpu.SemaphoreType.DMA((3, 2)),
            pltpu.SemaphoreType.DMA((2,)),
        ],
        compiler_params=params(52),
        name="finish",
    )(group_weights(), side_weights(), left, middle, right, edge_right, edge_left, coefs)


def solution(mesh):
    return jax.shard_map(
        local,
        mesh=mesh,
        in_specs=(
            P(("wide", "narrow"), None, None),
            P(("wide", "narrow")),
            P("wide", "narrow"),
            P("wide", "narrow"),
            P("wide", "narrow"),
            P("wide", "narrow"),
        ),
        out_specs=P("wide", "narrow"),
        check_vma=False,
    )
```

```python
import functools

import jax
import jax.numpy as jnp
import numpy as np
from jax import lax
from jax.experimental import pallas as pl
from jax.experimental.pallas import tpu as pltpu
from jax.sharding import PartitionSpec as P

OMEGA = 0.5
BS = 128
TOP = 16
BOTTOM = 24
F32 = jnp.float32
VMEM = pl.BlockSpec(memory_space=pltpu.VMEM)
SMEM = pl.BlockSpec(memory_space=pltpu.SMEM)
ANY = pl.BlockSpec(memory_space=pl.ANY)
HBM = pl.BlockSpec(memory_space=pltpu.HBM)


def lanes():
    return lax.broadcasted_iota(jnp.int32, (8, BS), 1)


def subs():
    return lax.broadcasted_iota(jnp.int32, (8, BS), 0)


def stage_kernel(a, b, l, head, tail, tiles, sems):
    rows = a.shape[0]
    copies = []
    for i, ref in enumerate((a, b, l)):
        copies.append(pltpu.make_async_copy(ref.at[0:8, :], tiles.at[i], sems.at[i]))
        copies.append(
            pltpu.make_async_copy(ref.at[rows - 8 : rows, :], tiles.at[3 + i], sems.at[3 + i])
        )
    for copy in copies:
        copy.start()
    for copy in copies:
        copy.wait()
    sub = lax.broadcasted_iota(jnp.int32, (8, a.shape[1]), 0)
    head[...] = jnp.where(
        sub < 3,
        tiles[0],
        jnp.where(sub < 6, pltpu.roll(tiles[1], 3, 0), pltpu.roll(tiles[2], 6, 0)),
    )
    tail[...] = jnp.where(
        sub < 3,
        pltpu.roll(tiles[3], 3, 0),
        jnp.where(sub < 6, pltpu.roll(tiles[4], 6, 0), tiles[5]),
    )


def rank_of(source, size):
    return source >> (size.bit_length() - 1) if size & (size - 1) == 0 else lax.div(source, size)


def rest_of(source, size):
    return source & (size - 1) if size & (size - 1) == 0 else lax.rem(source, size)


def source_of(table, groups, row, g):
    return table[row, g // (groups // 2), g % (groups // 2)]


def slot_of(owners, position):
    hit = jnp.int32(0)
    for earlier in range(position):
        hit = hit | (owners[earlier] == owners[position]).astype(jnp.int32)
    return hit


def send_kernel(dims, table, field, out, strip, sems, strip_sem):
    ranks, groups, per_device, segments = dims
    me = lax.axis_index("wide")
    picked, wanted = [], []

    def send(w, slot, local):
        return pltpu.make_async_copy(
            field.at[local], out.at[w, pl.ds(slot * BS, BS), :], sems.at[w, slot]
        )

    for w in range(ranks):
        low, high, any_hit = jnp.int32(0), jnp.int32(0), jnp.int32(0)
        sources = [source_of(table, groups, w, g) for g in range(groups)]
        hits = [rank_of(source, per_device * segments) == me for source in sources]
        for source, hit in zip(sources, hits):
            high = jnp.where(hit, source, high)
            any_hit = jnp.where(hit, 1, any_hit)
        for source, hit in zip(reversed(sources), reversed(hits)):
            low = jnp.where(hit, source, low)
        low, high = rest_of(low, per_device), rest_of(high, per_device)
        picked.append((low, high))
        wanted.append(any_hit)

        @pl.when(any_hit == 1)
        def _():
            send(w, 0, low).start()
            send(w, 1, high).start()

    sub = subs()
    for w in range(ranks):
        up, down = picked[max(w - 1, 0)], picked[min(w + 1, ranks - 1)]
        strip[w, 0:8, :] = jnp.where(
            sub < 4,
            pltpu.roll(field[up[0], BS - 8 : BS, :], 4, 0),
            field[up[1], BS - 8 : BS, :],
        )
        strip[w, 8:16, :] = jnp.where(
            sub < 4, field[down[0], 0:8, :], pltpu.roll(field[down[1], 0:8, :], 4, 0)
        )
    copy = pltpu.make_async_copy(strip, out.at[:, 2 * BS : 2 * BS + 16, :], strip_sem)
    copy.start()
    for w in range(ranks):

        @pl.when(wanted[w] == 1)
        def _():
            for slot in range(2):
                send(w, slot, 0).wait()

    copy.wait()


def take_kernel(dims, table, recv, left, middle, right, tiles, sems, tile_sems):
    ranks, groups, per_device, segments = dims
    gy_count = groups // 2
    me = lax.axis_index("wide")
    up, down = jnp.maximum(me - 1, 0), jnp.minimum(me + 1, ranks - 1)

    def owners_of(row):
        return [
            rank_of(source_of(table, groups, row, g), per_device * segments) for g in range(groups)
        ]

    mine, above, below = owners_of(me), owners_of(up), owners_of(down)

    def column(gy):
        if gy == 0:
            return left
        if gy == gy_count - 1:
            return right
        return middle.at[gy - 1]

    copies = []
    for gx in range(2):
        for gy in range(gy_count):
            g = gx * gy_count + gy
            start = pl.multiple_of(slot_of(mine, g) * BS, BS)
            copies.append(
                pltpu.make_async_copy(
                    recv.at[mine[g], pl.ds(start, BS), :],
                    column(gy).at[8 + gx * BS : 8 + (gx + 1) * BS, :],
                    sems.at[g],
                )
            )
    for gy in range(gy_count):
        copies.append(
            pltpu.make_async_copy(
                recv.at[above[gy_count + gy], 2 * BS : 2 * BS + 8, :],
                tiles.at[gy],
                tile_sems.at[gy],
            )
        )
        copies.append(
            pltpu.make_async_copy(
                recv.at[below[gy], 2 * BS + 8 : 2 * BS + 16, :],
                tiles.at[gy_count + gy],
                tile_sems.at[gy_count + gy],
            )
        )
    for copy in copies:
        copy.start()
    for copy in copies:
        copy.wait()
    for gy in range(gy_count):
        tile = tiles[gy]
        tile = jnp.where(slot_of(above, gy_count + gy) == 0, pltpu.roll(tile, 4, 0), tile)
        column(gy)[0:8, :] = jnp.where(me > 0, tile, 0.0)
        tile = tiles[gy_count + gy]
        tile = jnp.where(slot_of(below, gy) == 1, pltpu.roll(tile, 4, 0), tile)
        column(gy)[8 + 2 * BS : 16 + 2 * BS, :] = jnp.where(me < ranks - 1, tile, 0.0)


def turn(x, by):
    return pltpu.roll(x, by % BS, 1)


def swap_stage(tiles, bit, lane):
    high = (lane & bit) != 0
    partner = lane ^ bit
    done = list(tiles)
    for low in range(len(tiles)):
        if not low & bit:
            first, second = tiles[low], tiles[low | bit]
            moved = jnp.take_along_axis(jnp.where(high, first, second), partner, axis=1)
            done[low] = jnp.where(high, moved, first)
            done[low | bit] = jnp.where(high, second, moved)
    return done


def interleave(tiles, lane):
    for bit in (1, 2):
        tiles = swap_stage(tiles, bit, lane)
    return tiles


def right_of(ts, lane):
    side = ts[-1]
    source = jnp.where(lane < BS - 4, lane + 4, jnp.where(lane == BS - 1, 0, lane - (BS - 5)))
    done = []
    for first in range(0, len(ts) - 1, 4):
        group = ts[first : first + 4]
        edge = jnp.where(lane == 0, ts[first + 4], group[0])
        done += group[1:] + [jnp.take_along_axis(edge, source, axis=1)]
    return done + [turn(jnp.where(lane == 0, ts[0], side), -1)]


def left_of(ts, lane):
    side = ts[-1]
    source = jnp.where(lane >= 4, lane - 4, jnp.where(lane == 0, BS - 1, lane + (BS - 5)))
    done = []
    for first in range(0, len(ts) - 1, 4):
        group = ts[first : first + 4]
        edge = jnp.where(lane == BS - 1, ts[first - 1], group[3])
        done += [jnp.take_along_axis(edge, source, axis=1)] + group[:3]
    return done + [turn(jnp.where(lane == BS - 1, ts[-2], side), 1)]


def spacing(dims, table, row, g):
    _, groups, per_device, segments = dims
    source = source_of(table, groups, row, g)
    level = table[rank_of(source, per_device * segments), 2, rest_of(source, per_device)]
    return jnp.where(level >= 1, F32(4.0), F32(1.0))


def halo_rows(dims, above, below, rows):
    me, ranks = lax.axis_index("wide"), dims[0]
    up, down = jnp.maximum(me - 1, 0), jnp.minimum(me + 1, ranks - 1)
    return (
        (TOP - 8, above, up, dims[1] // 2, (5, 2, 0)),
        (TOP + rows, below, down, 0, (0, 5, 2)),
    )


def pack_kernel(dims, table, a_in, b_in, l_in, above, below, to_left, to_right, raw, sems):
    rows, columns = a_in.shape
    gy_count = dims[1] // 2
    me = lax.axis_index("wide")
    copies = []
    for i, ref in enumerate((a_in, b_in, l_in)):
        for side, first in enumerate((0, columns - BS)):
            copies.append(
                pltpu.make_async_copy(
                    ref.at[:, first : first + BS], raw.at[side, i], sems.at[side, i]
                )
            )
    for copy in copies:
        copy.start()
    lane = lanes()
    strips = rows // 8 + 2
    per_tile = BS // 8
    halos = halo_rows(dims, above, below, rows)

    def strip_of(k, side):
        gy = side * (gy_count - 1)
        first = side * (columns - BS)
        if 0 < k < strips - 1:
            s = own[2 * (k - 1) // (strips - 2)][side]
            a, b, l = [raw[side, i, 8 * (k - 1) : 8 * k, :] for i in range(3)]
        else:
            _, halo, base, at, turns = halos[0 if k == 0 else 1]
            s = spacing(dims, table, base, at + gy)
            a, b, l = [pltpu.roll(halo[:, first : first + BS], by, 0) for by in turns]
        return a * (0.5 * s), b * (s * s), l

    own = [
        [spacing(dims, table, me, gx * gy_count + side * (gy_count - 1)) for side in range(2)]
        for gx in range(2)
    ]
    for copy in copies:
        copy.wait()
    for side, out in ((0, to_left), (1, to_right)):
        sign = 1 - 2 * side
        for tile in range(out.shape[0] // 8):
            packed = jnp.zeros((8, BS), F32)
            for slot in range(per_tile):
                k = tile * per_tile + slot
                if k >= strips:
                    break
                place = (lane - 8 * slot) & (BS - 1)
                place = place if side == 0 else BS - 1 - place
                a, b, l = strip_of(k, side)
                packed = jnp.where(place < 3, turn(a, 8 * slot), packed)
                packed = jnp.where((place >= 3) & (place < 6), turn(b, 8 * slot + 3 * sign), packed)
                packed = jnp.where((place >= 6) & (place < 8), turn(l, 8 * slot + 6 * sign), packed)
            out[8 * tile : 8 * tile + 8, :] = packed


FX, FY, BEND, WEIGHT, LOAD = range(5)


def prep_kernel(
    dims, table, a_in, b_in, l_in, above, below, from_right, from_left, out, raw, a, kept, in_sems, out_sems
):
    ranks, groups, _, segments = dims
    gy_count = groups // 2
    planes = 2 * gy_count
    me, seg = lax.axis_index("wide"), lax.axis_index("narrow")
    rows = a_in.shape[0]
    chunks = in_sems.shape[1]
    size = rows // chunks
    lane, sub = lanes(), subs()
    strips = rows // 8 + 2
    near = lane < BS // 2
    cols = [slice(c * BS, (c + 1) * BS) for c in range(planes)]

    def read(i, chunk):
        ref = (a_in, b_in, l_in)[i]
        span = slice(chunk * size, (chunk + 1) * size)
        return pltpu.make_async_copy(ref.at[span, :], raw.at[i, span, :], in_sems.at[i, chunk])

    for chunk in range(chunks):
        for i in range(3):
            read(i, chunk).start()

    per_tile = BS // 8
    for k in range(strips):
        tile, slot = k // per_tile, k % per_tile
        at = slice(8 * tile, 8 * tile + 8)
        z = jnp.where(((lane - 8 * slot) & (BS - 1)) < 8, from_right[at, :], from_left[at, :])
        here = slice(TOP - 8 + 8 * k, TOP + 8 * k)
        a[planes, here, :] = turn(z, -8 * slot)
        kept[BEND, planes, here, :] = jnp.where(
            near, turn(z, -8 * slot - 3), turn(z, -8 * slot + 3)
        )
        kept[LOAD, planes, here, :] = jnp.where(
            near, turn(z, -8 * slot - 6), turn(z, -8 * slot + 6)
        )

    def put(row, *arrays):
        for out_ref, tiles in zip((a, kept.at[BEND], kept.at[LOAD]), arrays):
            for c, tile in enumerate(interleave(tiles, lane)):
                out_ref[c, pl.ds(row, 8), :] = tile

    for row, halo, base, at, turns in halo_rows(dims, above, below, rows):
        s = [spacing(dims, table, base, at + gy) for gy in range(gy_count)]
        put(
            row,
            [pltpu.roll(halo[:, cols[c]], turns[0], 0) * (0.5 * s[c // 2]) for c in range(planes)],
            [pltpu.roll(halo[:, cols[c]], turns[1], 0) * (s[c // 2] * s[c // 2]) for c in range(planes)],
            [pltpu.roll(halo[:, cols[c]], turns[2], 0) for c in range(planes)],
        )
    for chunk in range(chunks):
        gx = 2 * chunk // chunks
        s = [spacing(dims, table, me, gx * gy_count + gy) for gy in range(gy_count)]
        for i in range(3):
            read(i, chunk).wait()

        def lay(k, carry):
            row = pl.multiple_of(chunk * size + k * 8, 8)
            put(
                pl.multiple_of(row + TOP, 8),
                [raw[0, pl.ds(row, 8), cols[c]] * (0.5 * s[c // 2]) for c in range(planes)],
                [raw[1, pl.ds(row, 8), cols[c]] * (s[c // 2] * s[c // 2]) for c in range(planes)],
                [raw[2, pl.ds(row, 8), cols[c]] for c in range(planes)],
            )
            return carry

        lax.fori_loop(0, size // 8, lay, 0, unroll=4)

    parts = out_sems.shape[1]
    part_size = strips // parts

    def write(i, part):
        span = slice(TOP - 8 + 8 * part * part_size, TOP - 8 + 8 * (part + 1) * part_size)
        return pltpu.make_async_copy(
            kept.at[i, :, span, :], out.at[i, :, span, :], out_sems.at[i, part]
        )

    for part in range(parts):
        for i in (BEND, LOAD):
            write(i, part).start()
    side_ok = ((lane < 2) & (seg < segments - 1)) | ((lane >= BS - 2) & (seg > 0))
    b = kept.at[BEND]

    def step(k, carry):
        row = pl.multiple_of(TOP - 8 + 8 * k, 8)
        at = [a[c, pl.ds(row, 8), :] for c in range(planes + 1)]
        bt = [b[c, pl.ds(row, 8), :] for c in range(planes + 1)]
        face = [x + y for x, y in zip(at, right_of(at, lane))]
        face_l = left_of(face, lane)
        bt_r, bt_l = right_of(bt, lane), left_of(bt, lane)
        here = row + sub
        row_ok = ((here >= TOP) | (me > 0)) & ((here < TOP + rows) | (me < ranks - 1))
        for c in range(planes + 1):
            below_face = at[c] + a[c, pl.ds(row + 1, 8), :]
            above_face = at[c] + a[c, pl.ds(row - 1, 8), :]
            near_b = b[c, pl.ds(row + 1, 8), :] + b[c, pl.ds(row - 1, 8), :] + bt_r[c] + bt_l[c]
            diag = 16.0 * bt[c] + face[c] + face_l[c] + below_face + above_face + near_b
            ok = row_ok & side_ok if c == planes else row_ok
            kept[FX, c, pl.ds(row, 8), :] = face[c]
            kept[FY, c, pl.ds(row, 8), :] = below_face
            kept[WEIGHT, c, pl.ds(row, 8), :] = jnp.where(ok, OMEGA / diag, 0.0)
        return carry

    for part in range(parts):
        lax.fori_loop(part * part_size, (part + 1) * part_size, step, 0, unroll=11)
        for i in (FX, FY, WEIGHT):
            write(i, part).start()
    for part in range(parts):
        for i in range(5):
            write(i, part).wait()


def split3(x):
    high = x.astype(jnp.bfloat16)
    rest = x - high.astype(F32)
    mid = rest.astype(jnp.bfloat16)
    low = (rest - mid.astype(F32)).astype(jnp.bfloat16)
    return jnp.concatenate([high, mid, low], axis=1)


def refine_rows(sources, put, strips):
    sub = subs()

    def step(k, carry):
        row = pl.multiple_of(8 * k, 8)
        part = lax.rem(k, 8)
        top, bottom = (sub == 0) & (part == 1), (sub == 7) & (part == 0)
        for c, src in enumerate(sources):
            x = src[pl.ds(row + 8, 8), :]
            up = jnp.where(top, x, src[pl.ds(row + 7, 8), :])
            down = jnp.where(bottom, x, src[pl.ds(row + 9, 8), :])
            near = 0.75 * x
            put(c, row, near + 0.25 * up, near + 0.25 * down)
        return carry

    lax.fori_loop(0, strips, step, 0, unroll=2)


def finish_kernel(
    group_weights, side_weights, left, middle, right, from_right, from_left, k_in,
    out, cols, edge, v, m, h, v1, kept, early_sems, late_sems,
):
    planes = cols.shape[0]
    gy_count = planes // 2
    coarse = left.shape[0]
    rows = out.shape[0]
    lane = lanes()
    chunks = early_sems.shape[1]
    strips = rows // 8 + 2
    size = strips // chunks

    def early(i, chunk):
        span = slice(TOP - 8 + 8 * chunk * size, TOP - 8 + 8 * (chunk + 1) * size)
        return pltpu.make_async_copy(
            k_in.at[i, :, span, :], kept.at[i, :, span, :], early_sems.at[i, chunk]
        )

    def late(i):
        span = slice(TOP - 8, TOP - 8 + 8 * strips)
        return pltpu.make_async_copy(
            k_in.at[i, :, span, :], kept.at[i, :, span, :], late_sems.at[i - WEIGHT]
        )

    for chunk in range(chunks):
        for i in (FX, FY, BEND):
            early(i, chunk).start()
    for i in (WEIGHT, LOAD):
        late(i).start()

    for gy in range(gy_count):
        parent = left[...] if gy == 0 else right[...] if gy == gy_count - 1 else middle[gy - 1]
        wide = jnp.dot(split3(parent), group_weights[...], preferred_element_type=F32)
        for half in range(2):
            cols[2 * gy + half, 8 : 8 + coarse, :] = wide[:, half * BS : (half + 1) * BS]
    wide_lane = lax.broadcasted_iota(jnp.int32, (coarse, BS), 1)
    beside = jnp.where(wide_lane < BS // 2, from_right[...], from_left[...])
    edge[8 : 8 + coarse, :] = jnp.dot(
        split3(beside), side_weights[...], preferred_element_type=F32
    )

    def mix(k, carry):
        row = pl.multiple_of(8 + 8 * k, 8)
        tiles = [cols[c, pl.ds(row, 8), :] for c in range(planes)]
        for c, tile in enumerate(swap_stage(tiles, 2, lane)):
            cols[c, pl.ds(row, 8), :] = tile
        return carry

    lax.fori_loop(0, coarse // 8, mix, 0, unroll=2)

    def put(c, row, even, odd):
        v[c, pl.ds(2 * row, 8, stride=2), :] = even
        v[c, pl.ds(2 * row + 1, 8, stride=2), :] = odd

    refine_rows([cols.at[c] for c in range(planes)] + [edge], put, coarse // 8)

    fx, fy, b, wt, l = [kept.at[i] for i in range(5)]

    def moments(u, waits):
        def step(k, carry):
            row = pl.multiple_of(TOP - 8 + 8 * k, 8)
            t = [u[c, pl.ds(row, 8), :] for c in range(planes + 1)]
            dx = [r - x for r, x in zip(right_of(t, lane), t)]
            q = [fx[c, pl.ds(row, 8), :] * dx[c] for c in range(planes + 1)]
            dxl, ql = left_of(dx, lane), left_of(q, lane)
            for c in range(planes + 1):
                dyd = u[c, pl.ds(row + 1, 8), :] - t[c]
                dyu = t[c] - u[c, pl.ds(row - 1, 8), :]
                lap = (dx[c] - dxl[c]) + (dyd - dyu)
                m[c, pl.ds(row, 8), :] = b[c, pl.ds(row, 8), :] * lap
                h[c, pl.ds(row, 8), :] = (q[c] - ql[c]) + (
                    fy[c, pl.ds(row, 8), :] * dyd - fy[c, pl.ds(row - 1, 8), :] * dyu
                )
            return carry

        for chunk in range(chunks if waits else 1):
            first, last = 0, strips
            if waits:
                first, last = chunk * size, (chunk + 1) * size
                for i in (FX, FY, BEND):
                    early(i, chunk).wait()
            lax.fori_loop(first, last, step, 0, unroll=11)

    def update(first, count, u, put, width, unroll):
        def step(k, carry):
            row = pl.multiple_of(first + 8 * k, 8)
            t = [m[c, pl.ds(row, 8), :] for c in range(planes + 1)]
            tr, tl = right_of(t, lane), left_of(t, lane)
            new = []
            for c in range(width):
                lap = (
                    tr[c] + tl[c] + m[c, pl.ds(row - 1, 8), :] + m[c, pl.ds(row + 1, 8), :]
                ) - 4.0 * t[c]
                rest = (l[c, pl.ds(row, 8), :] + h[c, pl.ds(row, 8), :]) - lap
                new.append(u[c, pl.ds(row, 8), :] + wt[c, pl.ds(row, 8), :] * rest)
            put(row, new)
            return carry

        lax.fori_loop(0, count, step, 0, unroll=unroll)

    def put_middle(row, new):
        for c, value in enumerate(new):
            v1[c, pl.ds(row, 8), :] = value

    def put_out(row, new):
        at = pl.multiple_of(row - TOP, 8)
        for c, value in enumerate(interleave(new, lane)):
            out[pl.ds(at, 8), c * BS : (c + 1) * BS] = value

    moments(v, True)
    for i in (WEIGHT, LOAD):
        late(i).wait()
    update(TOP - 8, strips, v, put_middle, planes + 1, 11)
    moments(v1, False)
    update(TOP, rows // 8, v1, put_out, planes, 8)


def quadrant_table(half_index):
    half_size = BS // 2
    row_ids, col_ids = np.arange(BS)[:, None], np.arange(BS)[None, :]
    base_cell = half_index * half_size
    near_cell = base_cell + row_ids // 2
    other_cell = near_cell + np.where(row_ids % 2 == 1, 1, -1)
    other_cell = np.clip(other_cell, base_cell, base_cell + half_size - 1)
    return 0.75 * (col_ids == near_cell) + 0.25 * (col_ids == other_cell)


def group_weights():
    low, high = quadrant_table(0).T, quadrant_table(1).T
    both = np.stack([low, high], axis=1).reshape(BS, 2, BS // 2, 2)
    both = both.transpose(0, 3, 2, 1).reshape(BS, 2 * BS)
    return jnp.asarray(np.concatenate([both] * 3), jnp.bfloat16)


def side_weights():
    low, high = quadrant_table(0).T, quadrant_table(1).T
    rim = np.where(np.arange(BS)[None, :] < BS // 2, low, high)
    return jnp.asarray(np.concatenate([rim] * 3), jnp.bfloat16)


def params(limit_mib):
    return pltpu.CompilerParams(vmem_limit_bytes=int(limit_mib * (1 << 20)))


def shape(*dims):
    return jax.ShapeDtypeStruct(dims, F32)


def local(old_field, old_level, new_source, stretch_coef, bend_coef, load_field):
    per_device = old_field.shape[0]
    groups_x, groups_y = new_source.shape
    groups = groups_x * groups_y
    ranks, segments = lax.axis_size("wide"), lax.axis_size("narrow")
    dims = (ranks, groups, per_device, segments)
    rows, columns = load_field.shape
    planes = columns // BS
    tall = rows + TOP + BOTTOM
    coarse = 2 * BS + 16
    packet = 8 * -(-(rows // 8 + 2) // (BS // 8))
    up_links = [(i + 1, i) for i in range(ranks - 1)]
    down_links = [(i, i + 1) for i in range(ranks - 1)]
    left_links = [(i + 1, i) for i in range(segments - 1)]
    right_links = [(i, i + 1) for i in range(segments - 1)]

    facts = jnp.concatenate(
        [jnp.pad(new_source, ((0, 0), (0, per_device - groups_y))), old_level[None]]
    )
    table = lax.all_to_all(
        jnp.broadcast_to(facts[None], (ranks, *facts.shape)), "wide", 0, 0, tiled=True
    )

    head, tail = pl.pallas_call(
        stage_kernel,
        out_shape=[shape(8, columns), shape(8, columns)],
        in_specs=[HBM] * 3,
        out_specs=[VMEM] * 2,
        scratch_shapes=[pltpu.VMEM((6, 8, columns), F32), pltpu.SemaphoreType.DMA((6,))],
        compiler_params=params(52.3),
        name="stage_kernel",
    )(stretch_coef, bend_coef, load_field)
    above = lax.ppermute(tail, "wide", down_links)
    below = lax.ppermute(head, "wide", up_links)

    outgoing = pl.pallas_call(
        functools.partial(send_kernel, dims),
        out_shape=shape(ranks, coarse, BS),
        in_specs=[SMEM, VMEM],
        out_specs=HBM,
        scratch_shapes=[
            pltpu.VMEM((ranks, 16, BS), F32),
            pltpu.SemaphoreType.DMA((ranks, 2)),
            pltpu.SemaphoreType.DMA(()),
        ],
        compiler_params=params(52.3),
        name="send_build",
    )(table, old_field)
    incoming = lax.all_to_all(outgoing, "wide", 0, 0, tiled=True)

    to_left, to_right = pl.pallas_call(
        functools.partial(pack_kernel, dims),
        out_shape=[shape(packet, BS)] * 2,
        in_specs=[SMEM] + [HBM] * 3 + [VMEM] * 2,
        out_specs=[VMEM] * 2,
        scratch_shapes=[pltpu.VMEM((2, 3, rows, BS), F32), pltpu.SemaphoreType.DMA((2, 3))],
        compiler_params=params(52.3),
        name="pack",
    )(table, stretch_coef, bend_coef, load_field, above, below)
    from_right = lax.ppermute(to_left, "narrow", left_links)
    from_left = lax.ppermute(to_right, "narrow", right_links)
    coefs = pl.pallas_call(
        functools.partial(prep_kernel, dims),
        out_shape=shape(5, planes + 1, tall, BS),
        in_specs=[SMEM] + [HBM] * 3 + [VMEM] * 4,
        out_specs=HBM,
        scratch_shapes=[
            pltpu.VMEM((3, rows, columns), F32),
            pltpu.VMEM((planes + 1, tall, BS), F32),
            pltpu.VMEM((5, planes + 1, tall, BS), F32),
            pltpu.SemaphoreType.DMA((3, 4)),
            pltpu.SemaphoreType.DMA((5, 3)),
        ],
        compiler_params=params(52.3),
        name="prep_kernel",
    )(table, stretch_coef, bend_coef, load_field, above, below, from_right, from_left)

    left, middle, right = pl.pallas_call(
        functools.partial(take_kernel, dims),
        out_shape=[shape(coarse, BS), shape(groups_y - 2, coarse, BS), shape(coarse, BS)],
        in_specs=[SMEM, HBM],
        out_specs=[VMEM] * 3,
        scratch_shapes=[
            pltpu.VMEM((2 * groups_y, 8, BS), F32),
            pltpu.SemaphoreType.DMA((groups,)),
            pltpu.SemaphoreType.DMA((2 * groups_y,)),
        ],
        compiler_params=params(2),
        name="take",
    )(table, incoming)
    edge_right = lax.ppermute(left, "narrow", left_links)
    edge_left = lax.ppermute(right, "narrow", right_links)

    return pl.pallas_call(
        finish_kernel,
        out_shape=shape(rows, columns),
        in_specs=[VMEM] * 7 + [HBM],
        out_specs=VMEM,
        scratch_shapes=[
            pltpu.VMEM((planes, coarse + 16, BS), F32),
            pltpu.VMEM((coarse + 16, BS), F32),
        ]
        + [pltpu.VMEM((planes + 1, tall, BS), F32)] * 4
        + [
            pltpu.VMEM((5, planes + 1, tall, BS), F32),
            pltpu.SemaphoreType.DMA((3, 2)),
            pltpu.SemaphoreType.DMA((2,)),
        ],
        compiler_params=params(52),
        name="finish",
    )(group_weights(), side_weights(), left, middle, right, edge_right, edge_left, coefs)


def solution(mesh):
    return jax.shard_map(
        local,
        mesh=mesh,
        in_specs=(
            P(("wide", "narrow"), None, None),
            P(("wide", "narrow")),
            P("wide", "narrow"),
            P("wide", "narrow"),
            P("wide", "narrow"),
            P("wide", "narrow"),
        ),
        out_specs=P("wide", "narrow"),
        check_vma=False,
    )
```
